256 devices in a mesh: row: 32 (over x, z), col: 8 (over y, core).
Axes of the slice: x: 4, y: 4, z: 8, core: 2. Of those that a mesh axis runs over, the one named last changes fastest.
Arguments:
- h_blocks: bfloat16 [4, 32, 16, 128, 128], P(None, 'row', 'col'), may hold values from -1.1953125 to 1.1953125
- p_blocks: bfloat16 [4, 32, 16, 128, 128], P(None, 'row', 'col'), may hold values from -1.1953125 to 1.1953125
- p1_blocks: bfloat16 [4, 32, 16, 128, 128], P(None, 'row', 'col'), may hold values from -1.1953125 to 1.1953125
- h_mask: int32 [4, 32, 16], P(None, 'row', 'col'), may hold values 0 or 1
- p_mask: int32 [4, 32, 16], P(None, 'row', 'col'), may hold values 0 or 1
- p1_mask: int32 [4, 32, 16], P(None, 'row', 'col'), may hold values 0 or 1
Outputs:
- commutator: bfloat16 [4, 32, 16, 128, 128], P(None, 'row', 'col')
- response: bfloat16 [4, 32, 16, 128, 128], P(None, 'row', 'col')
The draws below stay inside these ranges and needn't reach their ends.
All inputs are finite; a program needn't handle non-finite values. No bound on the sum of `h_mask` or of `p_mask` or of `p1_mask` on one device may be relied on, other than what follows from the above.
Results may differ from the reference program's by a relative error of at most 0.001.
Values may be sent and summed in bfloat16 or wider, within the bound.
A program may use at most 128 MiB of HBM per device.

```python
import jax
import jax.numpy as jnp

B = 128
K = 16
ROWS_DEV = 4
ROW_OWNERS = 32
BLOCK_ROWS = 128
N_ROW = 32
N_COL = 8


def place_ends(entries, stream_key, low, largest):
    dims = entries.shape
    spot = [jax.random.randint(jax.random.fold_in(stream_key, axis), (), 0, dims[axis]) for axis in range(len(dims))]
    entries = entries.at[tuple(spot)].set(low)
    longest = dims.index(max(dims))
    spot[longest] = (spot[longest] + 1) % dims[longest]
    return entries.at[tuple(spot)].set(largest)


def block_levels(stream_key, extent, cuts, low, high):
    def one(axis_at, parts):
        heights = jax.random.uniform(jax.random.fold_in(jax.random.fold_in(stream_key, 6), axis_at), (parts,), jnp.float32, low / len(cuts), high / len(cuts))
        return jnp.repeat(jnp.exp(heights), extent[axis_at] // parts).reshape((-1,) + (1,) * (len(extent) - axis_at - 1))

    factor_of = one(*cuts[0])
    for cut in cuts[1:]:
        factor_of = factor_of * one(*cut)
    return factor_of


def normal_values(rng, extent, scale, bound, pieces=(), kind=jnp.bfloat16):
    result = scale * jax.random.normal(rng, extent, jnp.float32)
    if pieces:
        result = result * block_levels(rng, extent, pieces, -0.22, 0.18)
    return jnp.clip(result, -bound, bound).astype(kind)


def setup_inputs(seed: int = 0) -> dict:
    keys = jax.random.split(jax.random.key(seed), 7)
    return {
        "h_blocks": normal_values(keys[0], (ROWS_DEV, ROW_OWNERS, K, B, B), 0.2, 1.1953125, ((1, 32), (2, 8))),
        "p_blocks": normal_values(keys[1], (ROWS_DEV, ROW_OWNERS, K, B, B), 0.2, 1.1953125, ((1, 32), (2, 8))),
        "p1_blocks": normal_values(keys[2], (ROWS_DEV, ROW_OWNERS, K, B, B), 0.2, 1.1953125, ((1, 32), (2, 8))),
        "h_mask": place_ends((jax.random.randint(keys[3], (ROWS_DEV, ROW_OWNERS, K), 0, 4) < 3).astype(jnp.int32), jax.random.fold_in(keys[3], 1), 0, 1),
        "p_mask": place_ends((jax.random.randint(keys[4], (ROWS_DEV, ROW_OWNERS, K), 0, 4) < 3).astype(jnp.int32), jax.random.fold_in(keys[4], 1), 0, 1),
        "p1_mask": place_ends((jax.random.randint(keys[5], (ROWS_DEV, ROW_OWNERS, K), 0, 4) < 3).astype(jnp.int32), jax.random.fold_in(keys[5], 1), 0, 1),
    }


def band_layout():
    half_band = K // 2
    slot_count = K // N_COL
    local_row = jnp.arange(ROWS_DEV, dtype=jnp.int32)[:, None, None]
    owner_row = jnp.arange(N_ROW, dtype=jnp.int32)[None, :, None]
    slot_index = jnp.arange(K, dtype=jnp.int32)[None, None, :]
    block_row = owner_row + N_ROW * local_row + 0 * slot_index
    owner_col = slot_index // slot_count
    position = (owner_col - block_row + half_band) % N_COL + N_COL * (slot_index % slot_count)
    return block_row.astype(jnp.int32), position.astype(jnp.int32)


def to_band(values, pattern, block_row, position):
    kept_values = values * pattern[..., None, None].astype(values.dtype)
    return jnp.zeros((BLOCK_ROWS, K, B, B), values.dtype).at[block_row, position].set(kept_values)


def product(left_band, right_band):
    half_band = K // 2
    summed = jnp.zeros((BLOCK_ROWS, K, B, B), jnp.float32)
    for offset in range(-half_band, half_band):
        shifted = jnp.roll(right_band, -offset, axis=0)
        first_out = max(-half_band, offset - half_band)
        last_out = min(half_band - 1, offset + half_band - 1)
        left_column = left_band[:, offset + half_band].astype(jnp.float32)
        right_part = shifted[:, first_out - offset + half_band:last_out - offset + half_band + 1].astype(jnp.float32)
        partial_sum = jnp.einsum('qij,qtjl->qtil', left_column, right_part)
        summed = summed.at[:, first_out + half_band:last_out + half_band + 1].add(partial_sum)
    return summed


def reference(h_blocks, p_blocks, p1_blocks, h_mask, p_mask, p1_mask):
    block_row, position = band_layout()
    h_band = to_band(h_blocks, h_mask, block_row, position)
    p_band = to_band(p_blocks, p_mask, block_row, position)
    p1_band = to_band(p1_blocks, p1_mask, block_row, position)
    output_pattern = p1_mask[..., None, None].astype(jnp.float32)
    commuted = product(h_band, p1_band) - product(p1_band, h_band)
    purified = product(p_band, p1_band) + product(p1_band, p_band)
    commutator = (commuted[block_row, position] * output_pattern).astype(jnp.bfloat16)
    response = (purified[block_row, position] * output_pattern).astype(jnp.bfloat16)
    return commutator, response
```

```python
import functools

import jax
import jax.numpy as jnp
from jax import lax
from jax.experimental import pallas as pl
from jax.experimental.pallas import tpu as pltpu
from jax.sharding import PartitionSpec as P

MESH = pl.DeviceIdType.MESH
NX, NY, NZ, NC = 4, 4, 8, 2
NM = 4
M, O = 0, 1
UP_HOPS = (4, 3)
DOWN_HOPS = (3, 4)


def kernel(own, out_m, out_o, strip, left, far, out_f, acc,
           z_recv, z_send, l_recv, y_send, c_send, f_send, p_recv, p_send, q_send,
           r_send, r_recv, local_sem):
    row, col = lax.axis_index("row"), lax.axis_index("col")
    x, z = row // NZ, row % NZ
    y, k = col // NC, col % NC
    u = col
    low = z <= u
    x_up, x_dn = (x + 1) % NX, (x + NX - 1) % NX
    z_up, z_dn = (z + 1) % NZ, (z + NZ - 1) % NZ
    y_up, y_dn = (y + 1) % NY, (y + NY - 1) % NY

    def dev(x_=x, y_=y, z_=z, k_=k):
        return (x_ * NZ + z_, y_ * NC + k_)

    dev_zu, dev_zd = dev(z_=z_up), dev(z_=z_dn)
    dev_yu, dev_yd = dev(y_=y_up), dev(y_=y_dn)
    dev_xu, dev_xd = dev(x_=x_up), dev(x_=x_dn)
    dev_c = dev(k_=1 - k)

    def remote(src, dst, send, recv, device):
        return pltpu.make_async_remote_copy(
            src_ref=src, dst_ref=dst, send_sem=send, recv_sem=recv,
            device_id=device, device_id_type=MESH)

    barrier = pltpu.get_barrier_semaphore()
    for peer in (dev_zu, dev_zd, dev_yu, dev_yd, dev_xu, dev_xd, dev_c):
        pl.semaphore_signal(barrier, inc=1, device_id=peer, device_id_type=MESH)
    pl.semaphore_wait(barrier, 7)

    def z_copy(up, hop, kind, m):
        origin = (z - hop + NZ) % NZ if up else (z + hop) % NZ
        src = own.at[M, m] if (hop == 0 and kind == M) else strip.at[origin, kind, m]
        return remote(src, strip.at[origin, kind, m], z_send.at[0 if up else 1, hop, kind, m],
                      z_recv.at[origin, kind, m], dev_zu if up else dev_zd)

    def z_arrival(up, hop, kind, m):
        origin = (z - hop + NZ) % NZ if up else (z + hop) % NZ
        return remote(strip.at[origin, kind, m], strip.at[origin, kind, m],
                      z_send.at[0 if up else 1, 0, kind, m], z_recv.at[origin, kind, m], dev_c)

    def z_round(hop, kind):
        for m in range(NM):
            for up in (True, False):
                limit = (UP_HOPS if up else DOWN_HOPS)[kind]
                if hop <= limit:
                    z_arrival(up, hop, kind, m).wait_recv()
                    if hop < limit:
                        z_copy(up, hop, kind, m).start()

    for m in range(NM):
        z_copy(True, 0, M, m).start()
        z_copy(False, 0, M, m).start()

    dev_f = (jnp.where(low, x_dn, x_up) * NZ + z, col)
    shift_up = jnp.where(x == NX - 1, 1, 0)
    shift_dn = jnp.where(x == 0, NM - 1, 0)
    f_shift = jnp.where(low, shift_dn, shift_up)

    def f_copy(m):
        there = (m + f_shift) % NM
        return remote(own.at[O, m], strip.at[z, O, there], f_send.at[m], z_recv.at[z, O, there], dev_f)

    for m in range(NM):
        f_copy(m).start()

    def l_wait(who, kind):
        remote(left.at[who, kind], left.at[who, kind], c_send.at[0, 0], l_recv.at[who, kind], dev_c).wait_recv()

    def y_copy(slot, up, kind, relay):
        if relay:
            who = (y_dn if up else y_up) * NC + k
            src = left.at[who, kind]
        else:
            who = u
            src = own.at[kind]
        return remote(src, left.at[who, kind], y_send.at[slot], l_recv.at[who, kind], dev_yu if up else dev_yd)

    y_copies = [y_copy(0, True, M, False), y_copy(1, False, O, False),
                y_copy(2, True, O, False), y_copy(3, False, M, False),
                y_copy(4, True, M, True), y_copy(5, False, O, True)]
    for c in y_copies[:4]:
        c.start()

    def c_copy(d, kind):
        who = ((y + d) % NY) * NC + k
        src = own.at[kind] if d == 0 else left.at[who, kind]
        return remote(src, left.at[who, kind], c_send.at[d, kind], l_recv.at[who, kind], dev_c)

    c_copy(0, M).start()
    c_copy(0, O).start()
    keep_left = pltpu.make_async_copy(own, left.at[u], local_sem.at[0])
    keep_left.start()
    keep_strip = pltpu.make_async_copy(own.at[M], strip.at[z, M], local_sem.at[1])
    keep_strip.start()

    need = (2 * y + 1 >= z, 2 * y < z)

    def far_wanted(side, who, kind):
        if side == 0:
            inside = who >= z if kind == O else who <= 2 * y + 1
        else:
            inside = who < z if kind == O else who > 2 * y
        return jnp.logical_and(need[side], inside)

    def far_sends(d, kind, act):
        who = ((y + d) % NY) * NC + k
        src = own.at[kind] if d == 0 else left.at[who, kind]
        for side in (0, 1):
            @pl.when(far_wanted(side, who, kind))
            def _():
                shift = shift_dn if side == 0 else shift_up
                for m in range(NM):
                    act(remote(src.at[m], far.at[side, who, kind, (m + shift) % NM],
                               p_send.at[side, d, kind, m], p_recv.at[side, who, kind],
                               dev_xd if side == 0 else dev_xu))

    def far_pass(d, kind):
        who = ((y + d) % NY) * NC + k
        for side in (0, 1):
            @pl.when(far_wanted(side, who, kind))
            def _():
                spot = far.at[side, who, kind]
                remote(spot, spot, q_send.at[side, d, kind], p_recv.at[side, who, kind], dev_c).wait_recv()
                remote(spot, spot, q_send.at[side, d, kind], p_recv.at[side, who, kind], dev_c).start()

    def start(c):
        c.start()

    side_f = jnp.where(low, 0, 1)
    far_sends(0, M, start)

    for m in range(NM):
        remote(strip.at[z, O, m], strip.at[z, O, m], f_send.at[m], z_recv.at[z, O, m], dev_c).wait_recv()
        z_copy(True, 0, O, m).start()
        z_copy(False, 0, O, m).start()
    f_keep = pltpu.make_async_copy(strip.at[z, O], far.at[side_f, u, O], local_sem.at[2])
    f_keep.start()
    f_pass = remote(strip.at[z, O], far.at[side_f, u, O], local_sem.at[3], p_recv.at[side_f, u, O], dev_c)
    f_pass.start()

    l_wait(y_dn * NC + k, M)
    y_copies[4].start()
    far_sends(3, M, start)
    c_copy(3, M).start()
    l_wait(y_up * NC + k, O)
    y_copies[5].start()
    far_sends(1, O, start)
    c_copy(1, O).start()

    z_round(1, M)

    l_wait(y_dn * NC + k, O)
    far_sends(3, O, start)
    c_copy(3, O).start()
    l_wait(y_up * NC + k, M)
    far_sends(1, M, start)
    c_copy(1, M).start()

    z_round(1, O)
    far_pass(0, M)
    z_round(2, M)

    who2 = ((y + 2) % NY) * NC + k
    l_wait(who2, M)
    far_sends(2, M, start)
    c_copy(2, M).start()
    l_wait(who2, O)
    far_sends(2, O, start)
    c_copy(2, O).start()

    z_round(2, O)
    far_pass(3, M)
    far_pass(1, O)
    z_round(3, M)
    far_pass(3, O)
    far_pass(1, M)
    z_round(3, O)
    z_round(4, M)
    z_round(4, O)
    far_pass(2, M)
    far_pass(2, O)

    keep_left.wait()
    keep_strip.wait()
    f_keep.wait()
    for d in range(NY):
        who = ((y + d) % NY) * NC + 1 - k
        for kind in (M, O):
            l_wait(who, kind)
            for side in (0, 1):
                @pl.when(far_wanted(side, who, kind))
                def _():
                    spot = far.at[side, who, kind]
                    remote(spot, spot, q_send.at[side, d, kind], p_recv.at[side, who, kind], dev_c).wait_recv()

    r_shift = jnp.where(low, shift_up, shift_dn)
    dev_r = (jnp.where(low, x_up, x_dn) * NZ + z, col)

    def r_copy(m):
        there = (m + r_shift) % NM
        return remote(out_f.at[m], out_o.at[there], r_send.at[m], r_recv.at[there], dev_r)

    def per_plane(m, _):
        def per_row(zp, _):
            same = (zp <= u) == low
            valid_own = jnp.where(zp > u, zp >= z, zp < z)
            valid_far = jnp.where(low, zp >= z, zp < z)
            zero = jnp.zeros((128, 128), jnp.bfloat16)

            def pick(ok, block):
                return jnp.where(ok, block, zero)

            def rhs(kind):
                h, p1, p = (strip[zp, kind, m, i] for i in range(3))
                return h, p1, p

            hm, am, pm = rhs(M)
            hf, af, pf = rhs(O)
            w_c = jnp.concatenate([am, -hm, af, -hf], axis=0)
            w_r = jnp.concatenate([am, pm, af, pf], axis=0)
            lm = [left[zp, M, m, i] for i in range(3)]
            lo = [pick(valid_own, left[zp, O, m, i]) for i in range(3)]
            fo = [pick(valid_far, far[side_f, zp, O, m, i]) for i in range(3)]
            fm = [pick(same, far[side_f, zp, M, m, i]) for i in range(3)]

            def lhs(i):
                top = jnp.concatenate([lm[i], lm[1], lo[i], lo[1]], axis=1)
                low_part = jnp.concatenate([fo[i], fo[1], fm[i], fm[1]], axis=1)
                return jnp.concatenate([top, low_part], axis=0)

            acc[0] += jnp.dot(lhs(0), w_c, preferred_element_type=jnp.float32)
            acc[1] += jnp.dot(lhs(2), w_r, preferred_element_type=jnp.float32)
            return 0

        acc[...] = jnp.zeros_like(acc)
        lax.fori_loop(0, NZ, per_row, 0)
        for i in range(2):
            out_f[m, i] = acc[i, 128:].astype(jnp.bfloat16)
            out_m[m, i] = acc[i, :128].astype(jnp.bfloat16)
        r_copy(m).start()
        return 0

    lax.fori_loop(0, NM, per_plane, 0)

    for m in range(NM):
        r_copy(m).wait_send()
        remote(out_o.at[m], out_o.at[m], r_send.at[m], r_recv.at[m], dev_c).wait_recv()
        f_copy(m).wait_send()
        for kind in (M, O):
            for up in (True, False):
                for hop in range((UP_HOPS if up else DOWN_HOPS)[kind]):
                    z_copy(up, hop, kind, m).wait_send()
    for c in y_copies:
        c.wait_send()
    f_pass.wait_send()
    for d in range(NY):
        who = ((y + d) % NY) * NC + k
        for kind in (M, O):
            c_copy(d, kind).wait_send()
            if (d, kind) != (0, O):
                far_sends(d, kind, lambda c: c.wait_send())
                for side in (0, 1):
                    @pl.when(far_wanted(side, who, kind))
                    def _():
                        spot = far.at[side, who, kind]
                        remote(spot, spot, q_send.at[side, d, kind], p_recv.at[side, who, kind], dev_c).wait_send()


def exchange(own):
    dma = pltpu.SemaphoreType.DMA
    block = (128, 128)
    return pl.pallas_call(
        kernel,
        out_shape=(jax.ShapeDtypeStruct((NM, 2) + block, jnp.bfloat16),) * 2,
        in_specs=[pl.BlockSpec(memory_space=pltpu.VMEM)],
        out_specs=(pl.BlockSpec(memory_space=pltpu.VMEM),) * 2,
        scratch_shapes=[
            pltpu.VMEM((NZ, 2, NM, 3) + block, jnp.bfloat16),
            pltpu.VMEM((8, 2, NM, 3) + block, jnp.bfloat16),
            pltpu.VMEM((2, 8, 2, NM, 3) + block, jnp.bfloat16),
            pltpu.VMEM((NM, 2) + block, jnp.bfloat16),
            pltpu.VMEM((2, 256, 128), jnp.float32),
            dma((NZ, 2, NM)),
            dma((2, 4, 2, NM)),
            dma((8, 2)),
            dma((6,)),
            dma((NY, 2)),
            dma((NM,)),
            dma((2, 8, 2)),
            dma((2, NY, 2, NM)),
            dma((2, NY, 2)),
            dma((NM,)),
            dma((NM,)),
            dma((4,)),
        ],
        compiler_params=pltpu.CompilerParams(collective_id=0, has_side_effects=True),
        name="exchange",
    )(own)


def per_device(h_blocks, p_blocks, p1_blocks, h_mask, p_mask, p1_mask):
    row, col = lax.axis_index("row"), lax.axis_index("col")
    low = (row % NZ) <= col

    def masked(values, pattern):
        return values[:, 0] * pattern[:, 0][:, :, None, None].astype(values.dtype)

    blocks = jnp.stack((masked(h_blocks, h_mask), masked(p1_blocks, p1_mask), masked(p_blocks, p_mask)), axis=1)
    first, second = blocks[:, :, 0], blocks[:, :, 1]
    own = jnp.stack((jnp.where(low, second, first), jnp.where(low, first, second)))
    out_m, out_o = exchange(own)
    pattern = p1_mask[:, 0][:, :, None, None].astype(jnp.bfloat16)

    def placed(i):
        m, o = out_m[:, i], out_o[:, i]
        return (jnp.stack((jnp.where(low, o, m), jnp.where(low, m, o)), axis=1) * pattern)[:, None]

    return placed(0), placed(1)


def solution(mesh):
    blocks = P(None, "row", "col", None, None)
    masks = P(None, "row", "col")
    return jax.shard_map(
        per_device, mesh=mesh, in_specs=(blocks,) * 3 + (masks,) * 3,
        out_specs=(blocks, blocks), check_vma=False,
    )
```

```python
import functools

import jax
import jax.numpy as jnp
from jax import lax
from jax.experimental import pallas as pl
from jax.experimental.pallas import tpu as pltpu
from jax.sharding import PartitionSpec as P

MESH = pl.DeviceIdType.MESH
NX, NY, NZ, NC = 4, 4, 8, 2
NM = 4
M, O = 0, 1
UP_HOPS = (4, 3)
DOWN_HOPS = (3, 4)


def kernel(own, out_m, out_o, strip, left, far, out_f, acc,
           z_recv, z_send, l_recv, y_send, c_send, f_send, p_recv, p_send, q_send,
           fy_send, r_send, r_recv, local_sem):
    row, col = lax.axis_index("row"), lax.axis_index("col")
    x, z = row // NZ, row % NZ
    y, k = col // NC, col % NC
    u = col
    low = z <= u
    x_up, x_dn = (x + 1) % NX, (x + NX - 1) % NX
    z_up, z_dn = (z + 1) % NZ, (z + NZ - 1) % NZ
    y_up, y_dn = (y + 1) % NY, (y + NY - 1) % NY

    def dev(x_=x, y_=y, z_=z, k_=k):
        return (x_ * NZ + z_, y_ * NC + k_)

    dev_zu, dev_zd = dev(z_=z_up), dev(z_=z_dn)
    dev_yu, dev_yd = dev(y_=y_up), dev(y_=y_dn)
    dev_xu, dev_xd = dev(x_=x_up), dev(x_=x_dn)
    dev_c = dev(k_=1 - k)

    def remote(src, dst, send, recv, device):
        return pltpu.make_async_remote_copy(
            src_ref=src, dst_ref=dst, send_sem=send, recv_sem=recv,
            device_id=device, device_id_type=MESH)

    barrier = pltpu.get_barrier_semaphore()
    for peer in (dev_zu, dev_zd, dev_yu, dev_yd, dev_xu, dev_xd, dev_c):
        pl.semaphore_signal(barrier, inc=1, device_id=peer, device_id_type=MESH)
    pl.semaphore_wait(barrier, 7)

    def z_copy(up, hop, kind, m):
        origin = (z - hop + NZ) % NZ if up else (z + hop) % NZ
        src = own.at[M, m] if (hop == 0 and kind == M) else strip.at[origin, kind, m]
        return remote(src, strip.at[origin, kind, m], z_send.at[0 if up else 1, hop, kind, m],
                      z_recv.at[origin, kind, m], dev_zu if up else dev_zd)

    def z_arrival(up, hop, kind, m):
        origin = (z - hop + NZ) % NZ if up else (z + hop) % NZ
        return remote(strip.at[origin, kind, m], strip.at[origin, kind, m],
                      z_send.at[0 if up else 1, 0, kind, m], z_recv.at[origin, kind, m], dev_c)

    def z_round(hop, kind):
        for m in range(NM):
            for up in (True, False):
                limit = (UP_HOPS if up else DOWN_HOPS)[kind]
                if hop <= limit:
                    z_arrival(up, hop, kind, m).wait_recv()
                    if hop < limit:
                        z_copy(up, hop, kind, m).start()

    for m in range(NM):
        z_copy(True, 0, M, m).start()
        z_copy(False, 0, M, m).start()

    dev_f = (jnp.where(low, x_dn, x_up) * NZ + z, col)
    shift_up = jnp.where(x == NX - 1, 1, 0)
    shift_dn = jnp.where(x == 0, NM - 1, 0)
    f_shift = jnp.where(low, shift_dn, shift_up)

    def f_copy(m):
        there = (m + f_shift) % NM
        return remote(own.at[O, m], strip.at[z, O, there], f_send.at[m], z_recv.at[z, O, there], dev_f)

    for m in range(NM):
        f_copy(m).start()

    def l_wait(who, kind):
        remote(left.at[who, kind], left.at[who, kind], c_send.at[0, 0], l_recv.at[who, kind], dev_c).wait_recv()

    def y_copy(slot, up, kind, relay):
        if relay:
            who = (y_dn if up else y_up) * NC + k
            src = left.at[who, kind]
        else:
            who = u
            src = own.at[kind]
        return remote(src, left.at[who, kind], y_send.at[slot], l_recv.at[who, kind], dev_yu if up else dev_yd)

    y_copies = [y_copy(0, True, M, False), y_copy(1, False, O, False),
                y_copy(2, True, O, False), y_copy(3, False, M, False),
                y_copy(4, True, M, True), y_copy(5, False, O, True)]
    for c in y_copies[:4]:
        c.start()

    def c_copy(d, kind):
        who = ((y + d) % NY) * NC + k
        src = own.at[kind] if d == 0 else left.at[who, kind]
        return remote(src, left.at[who, kind], c_send.at[d, kind], l_recv.at[who, kind], dev_c)

    c_copy(0, M).start()
    c_copy(0, O).start()
    keep_left = pltpu.make_async_copy(own, left.at[u], local_sem.at[0])
    keep_left.start()
    keep_strip = pltpu.make_async_copy(own.at[M], strip.at[z, M], local_sem.at[1])
    keep_strip.start()

    def far_wanted(side, who, kind, at):
        if side == 0:
            inside = who >= z if kind == O else who <= 2 * at + 1
            return jnp.logical_and(2 * at + 1 >= z, inside)
        inside = who < z if kind == O else who > 2 * at
        return jnp.logical_and(2 * at < z, inside)

    def far_by_x(side, d, kind):
        home = (y + d) % NY
        who = home * NC + k
        wanted = far_wanted(side, who, kind, y)
        if d in (1, 3):
            wanted = jnp.logical_and(wanted, jnp.logical_not(far_wanted(side, who, kind, home)))
        return wanted

    def far_sends(d, kind, act):
        who = ((y + d) % NY) * NC + k
        src = own.at[kind] if d == 0 else left.at[who, kind]
        for side in (0, 1):
            @pl.when(far_by_x(side, d, kind))
            def _():
                shift = shift_dn if side == 0 else shift_up
                for m in range(NM):
                    act(remote(src.at[m], far.at[side, who, kind, (m + shift) % NM],
                               p_send.at[side, d, kind, m], p_recv.at[side, who, kind],
                               dev_xd if side == 0 else dev_xu))

    def far_y(kind, act):
        for side in (0, 1):
            for way, (there, device) in enumerate(((y_up, dev_yu), (y_dn, dev_yd))):
                @pl.when(jnp.logical_and(far_wanted(side, u, kind, y), far_wanted(side, u, kind, there)))
                def _():
                    src = strip.at[z, O] if kind == O else far.at[side, u, M]
                    act(remote(src, far.at[side, u, kind], fy_send.at[side, way, kind],
                               p_recv.at[side, u, kind], device))

    def far_pass(d, kind):
        who = ((y + d) % NY) * NC + k
        for side in (0, 1):
            @pl.when(far_wanted(side, who, kind, y))
            def _():
                spot = far.at[side, who, kind]
                remote(spot, spot, q_send.at[side, d, kind], p_recv.at[side, who, kind], dev_c).wait_recv()
                remote(spot, spot, q_send.at[side, d, kind], p_recv.at[side, who, kind], dev_c).start()

    def start(c):
        c.start()

    side_f = jnp.where(low, 0, 1)
    far_sends(0, M, start)

    for m in range(NM):
        remote(strip.at[z, O, m], strip.at[z, O, m], f_send.at[m], z_recv.at[z, O, m], dev_c).wait_recv()
        z_copy(True, 0, O, m).start()
        z_copy(False, 0, O, m).start()
    f_keep = pltpu.make_async_copy(strip.at[z, O], far.at[side_f, u, O], local_sem.at[2])
    f_keep.start()
    f_pass = remote(strip.at[z, O], far.at[side_f, u, O], local_sem.at[3], p_recv.at[side_f, u, O], dev_c)
    f_pass.start()

    l_wait(y_dn * NC + k, M)
    y_copies[4].start()
    far_sends(3, M, start)
    c_copy(3, M).start()
    l_wait(y_up * NC + k, O)
    y_copies[5].start()
    far_sends(1, O, start)
    c_copy(1, O).start()
    far_y(O, start)

    z_round(1, M)

    l_wait(y_dn * NC + k, O)
    far_sends(3, O, start)
    c_copy(3, O).start()
    l_wait(y_up * NC + k, M)
    far_sends(1, M, start)
    c_copy(1, M).start()

    far_pass(0, M)
    far_y(M, start)
    z_round(1, O)
    z_round(2, M)

    who2 = ((y + 2) % NY) * NC + k
    l_wait(who2, M)
    far_sends(2, M, start)
    c_copy(2, M).start()
    l_wait(who2, O)
    far_sends(2, O, start)
    c_copy(2, O).start()

    z_round(2, O)
    far_pass(3, O)
    far_pass(1, O)
    z_round(3, M)
    far_pass(3, M)
    far_pass(1, M)
    far_pass(2, M)
    z_round(3, O)
    far_pass(2, O)

    keep_left.wait()
    keep_strip.wait()
    f_keep.wait()
    for d in range(NY):
        who = ((y + d) % NY) * NC + 1 - k
        for kind in (M, O):
            l_wait(who, kind)
            for side in (0, 1):
                @pl.when(far_wanted(side, who, kind, y))
                def _():
                    spot = far.at[side, who, kind]
                    remote(spot, spot, q_send.at[side, d, kind], p_recv.at[side, who, kind], dev_c).wait_recv()

    r_shift = jnp.where(low, shift_up, shift_dn)
    dev_r = (jnp.where(low, x_up, x_dn) * NZ + z, col)

    def r_copy(m):
        there = (m + r_shift) % NM
        return remote(out_f.at[m], out_o.at[there], r_send.at[m], r_recv.at[there], dev_r)

    zero = jnp.zeros((128, 128), jnp.bfloat16)

    def pick(ok, block):
        return jnp.where(ok, block, zero)

    def products(m, zp):
        same = (zp <= u) == low
        valid_own = jnp.where(zp > u, zp >= z, zp < z)
        valid_far = jnp.where(low, zp >= z, zp < z)
        hm, am, pm = (strip[zp, M, m, i] for i in range(3))
        hf, af, pf = (strip[zp, O, m, i] for i in range(3))
        w_c = jnp.concatenate([am, -hm, af, -hf], axis=0)
        w_r = jnp.concatenate([am, pm, af, pf], axis=0)
        lm = [left[zp, M, m, i] for i in range(3)]
        lo = [pick(valid_own, left[zp, O, m, i]) for i in range(3)]
        fo = [pick(valid_far, far[side_f, zp, O, m, i]) for i in range(3)]
        fm = [pick(same, far[side_f, zp, M, m, i]) for i in range(3)]

        def lhs(i):
            top = jnp.concatenate([lm[i], lm[1], lo[i], lo[1]], axis=1)
            low_part = jnp.concatenate([fo[i], fo[1], fm[i], fm[1]], axis=1)
            return jnp.concatenate([top, low_part], axis=0)

        return (jnp.dot(lhs(0), w_c, preferred_element_type=jnp.float32),
                jnp.dot(lhs(2), w_r, preferred_element_type=jnp.float32))

    def add(m, zp):
        c, r = products(m, zp)
        acc[m, 0] += c
        acc[m, 1] += r

    for m in range(NM):
        acc[m] = jnp.zeros((2, 256, 128), jnp.float32)

    def early(i, _):
        d = i % (NZ - 1)
        add(i // (NZ - 1), (z + jnp.where(d > 3, d + 1, d)) % NZ)
        return 0

    lax.fori_loop(0, NM * (NZ - 1), early, 0)

    for m in range(NM):
        z_arrival(True, 4, M, m).wait_recv()
        z_arrival(False, 4, O, m).wait_recv()
        c, r = products(m, (z + 4) % NZ)
        c, r = c + acc[m, 0], r + acc[m, 1]
        out_f[m, 0] = c[128:].astype(jnp.bfloat16)
        out_f[m, 1] = r[128:].astype(jnp.bfloat16)
        out_m[m, 0] = c[:128].astype(jnp.bfloat16)
        out_m[m, 1] = r[:128].astype(jnp.bfloat16)
        r_copy(m).start()

    for m in range(NM):
        r_copy(m).wait_send()
        remote(out_o.at[m], out_o.at[m], r_send.at[m], r_recv.at[m], dev_c).wait_recv()
        f_copy(m).wait_send()
        for kind in (M, O):
            for up in (True, False):
                for hop in range((UP_HOPS if up else DOWN_HOPS)[kind]):
                    z_copy(up, hop, kind, m).wait_send()
    for c in y_copies:
        c.wait_send()
    f_pass.wait_send()
    far_y(M, lambda c: c.wait_send())
    far_y(O, lambda c: c.wait_send())
    for d in range(NY):
        who = ((y + d) % NY) * NC + k
        for kind in (M, O):
            c_copy(d, kind).wait_send()
            if (d, kind) != (0, O):
                far_sends(d, kind, lambda c: c.wait_send())
                for side in (0, 1):
                    @pl.when(far_wanted(side, who, kind, y))
                    def _():
                        spot = far.at[side, who, kind]
                        remote(spot, spot, q_send.at[side, d, kind], p_recv.at[side, who, kind], dev_c).wait_send()


def exchange(own):
    dma = pltpu.SemaphoreType.DMA
    block = (128, 128)
    return pl.pallas_call(
        kernel,
        out_shape=(jax.ShapeDtypeStruct((NM, 2) + block, jnp.bfloat16),) * 2,
        in_specs=[pl.BlockSpec(memory_space=pltpu.VMEM)],
        out_specs=(pl.BlockSpec(memory_space=pltpu.VMEM),) * 2,
        scratch_shapes=[
            pltpu.VMEM((NZ, 2, NM, 3) + block, jnp.bfloat16),
            pltpu.VMEM((8, 2, NM, 3) + block, jnp.bfloat16),
            pltpu.VMEM((2, 8, 2, NM, 3) + block, jnp.bfloat16),
            pltpu.VMEM((NM, 2) + block, jnp.bfloat16),
            pltpu.VMEM((NM, 2, 256, 128), jnp.float32),
            dma((NZ, 2, NM)),
            dma((2, 4, 2, NM)),
            dma((8, 2)),
            dma((6,)),
            dma((NY, 2)),
            dma((NM,)),
            dma((2, 8, 2)),
            dma((2, NY, 2, NM)),
            dma((2, NY, 2)),
            dma((2, 2, 2)),
            dma((NM,)),
            dma((NM,)),
            dma((4,)),
        ],
        compiler_params=pltpu.CompilerParams(collective_id=0, has_side_effects=True),
        name="exchange",
    )(own)


def per_device(h_blocks, p_blocks, p1_blocks, h_mask, p_mask, p1_mask):
    row, col = lax.axis_index("row"), lax.axis_index("col")
    low = (row % NZ) <= col

    def masked(values, pattern):
        return values[:, 0] * pattern[:, 0][:, :, None, None].astype(values.dtype)

    blocks = jnp.stack((masked(h_blocks, h_mask), masked(p1_blocks, p1_mask), masked(p_blocks, p_mask)), axis=1)
    first, second = blocks[:, :, 0], blocks[:, :, 1]
    own = jnp.stack((jnp.where(low, second, first), jnp.where(low, first, second)))
    out_m, out_o = exchange(own)
    pattern = p1_mask[:, 0][:, :, None, None].astype(jnp.bfloat16)

    def placed(i):
        m, o = out_m[:, i], out_o[:, i]
        return (jnp.stack((jnp.where(low, o, m), jnp.where(low, m, o)), axis=1) * pattern)[:, None]

    return placed(0), placed(1)


def solution(mesh):
    blocks = P(None, "row", "col", None, None)
    masks = P(None, "row", "col")
    return jax.shard_map(
        per_device, mesh=mesh, in_specs=(blocks,) * 3 + (masks,) * 3,
        out_specs=(blocks, blocks), check_vma=False,
    )
```

```python
import functools

import jax
import jax.numpy as jnp
from jax import lax
from jax.experimental import pallas as pl
from jax.experimental.pallas import tpu as pltpu
from jax.sharding import PartitionSpec as P

MESH = pl.DeviceIdType.MESH
NX, NY, NZ, NC = 4, 4, 8, 2
NM = 4
M, O = 0, 1
UP_HOPS = (4, 3)
DOWN_HOPS = (3, 4)


def kernel(h_ref, p1_ref, p_ref, h_mask, p1_mask, p_mask, out_c, out_r, raw, strip, left, far, out_f, back, acc,
           z_recv, z_send, l_recv, y_send, c_send, f_send, p_recv, p_send, q_send,
           fy_send, r_send, r_recv, local_sem):
    row, col = lax.axis_index("row"), lax.axis_index("col")
    x, z = row // NZ, row % NZ
    y, k = col // NC, col % NC
    u = col
    low = z <= u
    x_up, x_dn = (x + 1) % NX, (x + NX - 1) % NX
    z_up, z_dn = (z + 1) % NZ, (z + NZ - 1) % NZ
    y_up, y_dn = (y + 1) % NY, (y + NY - 1) % NY

    def dev(x_=x, y_=y, z_=z, k_=k):
        return (x_ * NZ + z_, y_ * NC + k_)

    dev_zu, dev_zd = dev(z_=z_up), dev(z_=z_dn)
    dev_yu, dev_yd = dev(y_=y_up), dev(y_=y_dn)
    dev_xu, dev_xd = dev(x_=x_up), dev(x_=x_dn)
    dev_c = dev(k_=1 - k)

    def remote(src, dst, send, recv, device):
        return pltpu.make_async_remote_copy(
            src_ref=src, dst_ref=dst, send_sem=send, recv_sem=recv,
            device_id=device, device_id_type=MESH)

    barrier = pltpu.get_barrier_semaphore()
    for peer in (dev_zu, dev_zd, dev_yu, dev_yd, dev_xu, dev_xd, dev_c):
        pl.semaphore_signal(barrier, inc=1, device_id=peer, device_id_type=MESH)

    slot_m = jnp.where(low, 1, 0)
    slots = (slot_m, 1 - slot_m)
    loads = [pltpu.make_async_copy(ref, raw.at[i], local_sem.at[i]) for i, ref in enumerate((h_ref, p1_ref, p_ref))]
    for c in loads:
        c.start()
    for m in range(NM):
        acc[m] = jnp.zeros((2, 2, 128, 128), jnp.float32)
    for i, (c, mask) in enumerate(zip(loads, (h_mask, p1_mask, p_mask))):
        c.wait()
        for kind in (M, O):
            for m in range(NM):
                keep = mask[slots[kind], m].astype(jnp.float32)
                block = (raw[i, m, slots[kind]].astype(jnp.float32) * keep).astype(jnp.bfloat16)
                left[u, kind, m, i] = block
                if kind == M:
                    strip[z, M, m, i] = block
    own = left.at[u]
    pl.semaphore_wait(barrier, 7)

    def z_copy(up, hop, kind, m):
        origin = (z - hop + NZ) % NZ if up else (z + hop) % NZ
        return remote(strip.at[origin, kind, m], strip.at[origin, kind, m], z_send.at[0 if up else 1, hop, kind, m],
                      z_recv.at[origin, kind, m], dev_zu if up else dev_zd)

    def z_arrival(up, hop, kind, m):
        origin = (z - hop + NZ) % NZ if up else (z + hop) % NZ
        return remote(strip.at[origin, kind, m], strip.at[origin, kind, m],
                      z_send.at[0 if up else 1, 0, kind, m], z_recv.at[origin, kind, m], dev_c)

    def z_round(hop, kind):
        for m in range(NM):
            for up in (True, False):
                limit = (UP_HOPS if up else DOWN_HOPS)[kind]
                if hop <= limit:
                    z_arrival(up, hop, kind, m).wait_recv()
                    if hop < limit:
                        z_copy(up, hop, kind, m).start()

    for m in range(NM):
        z_copy(True, 0, M, m).start()
        z_copy(False, 0, M, m).start()

    dev_f = (jnp.where(low, x_dn, x_up) * NZ + z, col)
    shift_up = jnp.where(x == NX - 1, 1, 0)
    shift_dn = jnp.where(x == 0, NM - 1, 0)
    f_shift = jnp.where(low, shift_dn, shift_up)

    def f_copy(m):
        there = (m + f_shift) % NM
        return remote(own.at[O, m], strip.at[z, O, there], f_send.at[m], z_recv.at[z, O, there], dev_f)

    for m in range(NM):
        f_copy(m).start()

    def l_wait(who, kind):
        remote(left.at[who, kind], left.at[who, kind], c_send.at[0, 0], l_recv.at[who, kind], dev_c).wait_recv()

    def y_copy(slot, up, kind, relay):
        if relay:
            who = (y_dn if up else y_up) * NC + k
            src = left.at[who, kind]
        else:
            who = u
            src = own.at[kind]
        return remote(src, left.at[who, kind], y_send.at[slot], l_recv.at[who, kind], dev_yu if up else dev_yd)

    y_copies = [y_copy(0, True, M, False), y_copy(1, False, O, False),
                y_copy(2, True, O, False), y_copy(3, False, M, False),
                y_copy(4, True, M, True), y_copy(5, False, O, True)]
    for c in y_copies[:4]:
        c.start()

    def c_copy(d, kind):
        who = ((y + d) % NY) * NC + k
        src = own.at[kind] if d == 0 else left.at[who, kind]
        return remote(src, left.at[who, kind], c_send.at[d, kind], l_recv.at[who, kind], dev_c)

    c_copy(0, M).start()
    c_copy(0, O).start()

    def far_wanted(side, who, kind, at):
        if side == 0:
            inside = who >= z if kind == O else who <= 2 * at + 1
            return jnp.logical_and(2 * at + 1 >= z, inside)
        inside = who < z if kind == O else who > 2 * at
        return jnp.logical_and(2 * at < z, inside)

    def far_by_x(side, d, kind):
        home = (y + d) % NY
        who = home * NC + k
        wanted = far_wanted(side, who, kind, y)
        if d in (1, 3):
            wanted = jnp.logical_and(wanted, jnp.logical_not(far_wanted(side, who, kind, home)))
        return wanted

    def far_sends(d, kind, act):
        who = ((y + d) % NY) * NC + k
        src = own.at[kind] if d == 0 else left.at[who, kind]
        for side in (0, 1):
            @pl.when(far_by_x(side, d, kind))
            def _():
                shift = shift_dn if side == 0 else shift_up
                for m in range(NM):
                    act(remote(src.at[m], far.at[side, who, kind, (m + shift) % NM],
                               p_send.at[side, d, kind, m], p_recv.at[side, who, kind],
                               dev_xd if side == 0 else dev_xu))

    def far_y(kind, act):
        for side in (0, 1):
            for way, (there, device) in enumerate(((y_up, dev_yu), (y_dn, dev_yd))):
                @pl.when(jnp.logical_and(far_wanted(side, u, kind, y), far_wanted(side, u, kind, there)))
                def _():
                    src = strip.at[z, O] if kind == O else far.at[side, u, M]
                    act(remote(src, far.at[side, u, kind], fy_send.at[side, way, kind],
                               p_recv.at[side, u, kind], device))

    def far_pass(d, kind):
        who = ((y + d) % NY) * NC + k
        for side in (0, 1):
            @pl.when(far_wanted(side, who, kind, y))
            def _():
                spot = far.at[side, who, kind]
                remote(spot, spot, q_send.at[side, d, kind], p_recv.at[side, who, kind], dev_c).wait_recv()
                remote(spot, spot, q_send.at[side, d, kind], p_recv.at[side, who, kind], dev_c).start()

    def start(c):
        c.start()

    side_f = jnp.where(low, 0, 1)
    far_sends(0, M, start)

    for m in range(NM):
        remote(strip.at[z, O, m], strip.at[z, O, m], f_send.at[m], z_recv.at[z, O, m], dev_c).wait_recv()
        z_copy(True, 0, O, m).start()
        z_copy(False, 0, O, m).start()
    f_keep = pltpu.make_async_copy(strip.at[z, O], far.at[side_f, u, O], local_sem.at[3])
    f_keep.start()
    f_pass = remote(strip.at[z, O], far.at[side_f, u, O], local_sem.at[4], p_recv.at[side_f, u, O], dev_c)
    f_pass.start()

    l_wait(y_dn * NC + k, M)
    y_copies[4].start()
    far_sends(3, M, start)
    c_copy(3, M).start()
    l_wait(y_up * NC + k, O)
    y_copies[5].start()
    far_sends(1, O, start)
    c_copy(1, O).start()
    far_y(O, start)

    z_round(1, M)

    l_wait(y_dn * NC + k, O)
    far_sends(3, O, start)
    c_copy(3, O).start()
    l_wait(y_up * NC + k, M)
    far_sends(1, M, start)
    c_copy(1, M).start()

    far_pass(0, M)
    far_y(M, start)
    z_round(1, O)
    z_round(2, M)

    who2 = ((y + 2) % NY) * NC + k
    l_wait(who2, M)
    far_sends(2, M, start)
    c_copy(2, M).start()
    l_wait(who2, O)
    far_sends(2, O, start)
    c_copy(2, O).start()

    z_round(2, O)
    far_pass(3, O)
    far_pass(1, O)

    zero = jnp.zeros((128, 128), jnp.bfloat16)

    def products(r, m, zp):
        hm, am, pm = (strip[zp, M, m, i] for i in range(3))
        hf, af, pf = (strip[zp, O, m, i] for i in range(3))
        if r == 0:
            ok = jnp.where(zp > u, zp >= z, zp < z)
            first = [left[zp, M, m, i] for i in range(3)]
            second = [jnp.where(ok, left[zp, O, m, i], zero) for i in range(3)]
        else:
            ok_m = jnp.where(low, zp >= z, zp < z)
            ok_f = (zp <= u) == low
            first = [jnp.where(ok_m, far[side_f, zp, O, m, i], zero) for i in range(3)]
            second = [jnp.where(ok_f, far[side_f, zp, M, m, i], zero) for i in range(3)]
        lh, la, lp = (jnp.concatenate([f, s], axis=1) for f, s in zip(first, second))
        one = jnp.dot(jnp.concatenate([lh, lp], axis=0), jnp.concatenate([am, af], axis=0),
                      preferred_element_type=jnp.float32)
        rhs = jnp.concatenate([jnp.concatenate([-hm, pm], axis=1), jnp.concatenate([-hf, pf], axis=1)], axis=0)
        two = jnp.dot(la, rhs, preferred_element_type=jnp.float32)
        return one[:128] + two[:, :128], one[128:] + two[:, 128:]

    def add(r, m, zp):
        c, s = products(r, m, zp)
        acc[m, r, 0] += c
        acc[m, r, 1] += s

    for d in range(NY):
        for kind in (M, O):
            l_wait(((y + d) % NY) * NC + 1 - k, kind)

    def near(i, _):
        add(0, i // 5, (z + i % 5 + 6) % NZ)
        return 0

    lax.fori_loop(0, NM * 5, near, 0)

    z_round(3, M)
    far_pass(3, M)
    far_pass(1, M)
    far_pass(2, M)
    z_round(3, O)
    far_pass(2, O)

    def third(i, _):
        add(0, i // 2, (z + 3 + 2 * (i % 2)) % NZ)
        return 0

    lax.fori_loop(0, NM * 2, third, 0)

    f_keep.wait()
    for d in range(NY):
        who = ((y + d) % NY) * NC + 1 - k
        for kind in (M, O):
            for side in (0, 1):
                @pl.when(far_wanted(side, who, kind, y))
                def _():
                    spot = far.at[side, who, kind]
                    remote(spot, spot, q_send.at[side, d, kind], p_recv.at[side, who, kind], dev_c).wait_recv()

    r_shift = jnp.where(low, shift_up, shift_dn)
    dev_r = (jnp.where(low, x_up, x_dn) * NZ + z, col)

    def r_copy(m):
        there = (m + r_shift) % NM
        return remote(out_f.at[m], back.at[there], r_send.at[m], r_recv.at[there], dev_r)

    def put(m, kind, c, s):
        keep = p1_mask[slots[kind], m].astype(jnp.float32)
        out_c[m, slots[kind]] = (c * keep).astype(jnp.bfloat16)
        out_r[m, slots[kind]] = (s * keep).astype(jnp.bfloat16)

    for m in range(NM):
        def early(i, _):
            add(1, m, (z + i + 5) % NZ)
            return 0

        lax.fori_loop(0, NZ - 1, early, 0)
        z_arrival(True, 4, M, m).wait_recv()
        z_arrival(False, 4, O, m).wait_recv()
        c, s = products(1, m, (z + 4) % NZ)
        out_f[m, 0] = (c + acc[m, 1, 0]).astype(jnp.bfloat16)
        out_f[m, 1] = (s + acc[m, 1, 1]).astype(jnp.bfloat16)
        c, s = products(0, m, (z + 4) % NZ)
        put(m, M, c + acc[m, 0, 0], s + acc[m, 0, 1])
        r_copy(m).start()

    for m in range(NM):
        remote(back.at[m], back.at[m], r_send.at[m], r_recv.at[m], dev_c).wait_recv()
        put(m, O, back[m, 0].astype(jnp.float32), back[m, 1].astype(jnp.float32))

    for m in range(NM):
        r_copy(m).wait_send()
        f_copy(m).wait_send()
        for kind in (M, O):
            for up in (True, False):
                for hop in range((UP_HOPS if up else DOWN_HOPS)[kind]):
                    z_copy(up, hop, kind, m).wait_send()
    for c in y_copies:
        c.wait_send()
    f_pass.wait_send()
    far_y(M, lambda c: c.wait_send())
    far_y(O, lambda c: c.wait_send())
    for d in range(NY):
        who = ((y + d) % NY) * NC + k
        for kind in (M, O):
            c_copy(d, kind).wait_send()
            if (d, kind) != (0, O):
                far_sends(d, kind, lambda c: c.wait_send())
                for side in (0, 1):
                    @pl.when(far_wanted(side, who, kind, y))
                    def _():
                        spot = far.at[side, who, kind]
                        remote(spot, spot, q_send.at[side, d, kind], p_recv.at[side, who, kind], dev_c).wait_send()


def exchange(values, masks):
    dma = pltpu.SemaphoreType.DMA
    block = (128, 128)
    return pl.pallas_call(
        kernel,
        out_shape=(jax.ShapeDtypeStruct((NM, 2) + block, jnp.bfloat16),) * 2,
        in_specs=[pl.BlockSpec(memory_space=pl.ANY)] * 3 + [pl.BlockSpec(memory_space=pltpu.SMEM)] * 3,
        out_specs=(pl.BlockSpec(memory_space=pltpu.VMEM),) * 2,
        scratch_shapes=[
            pltpu.VMEM((3, NM, 2) + block, jnp.bfloat16),
            pltpu.VMEM((NZ, 2, NM, 3) + block, jnp.bfloat16),
            pltpu.VMEM((8, 2, NM, 3) + block, jnp.bfloat16),
            pltpu.VMEM((2, 8, 2, NM, 3) + block, jnp.bfloat16),
            pltpu.VMEM((NM, 2) + block, jnp.bfloat16),
            pltpu.VMEM((NM, 2) + block, jnp.bfloat16),
            pltpu.VMEM((NM, 2, 2) + block, jnp.float32),
            dma((NZ, 2, NM)),
            dma((2, 4, 2, NM)),
            dma((8, 2)),
            dma((6,)),
            dma((NY, 2)),
            dma((NM,)),
            dma((2, 8, 2)),
            dma((2, NY, 2, NM)),
            dma((2, NY, 2)),
            dma((2, 2, 2)),
            dma((NM,)),
            dma((NM,)),
            dma((5,)),
        ],
        compiler_params=pltpu.CompilerParams(collective_id=0, has_side_effects=True),
        name="exchange",
    )(*values, *masks)


def per_device(h_blocks, p_blocks, p1_blocks, h_mask, p_mask, p1_mask):
    values = [v[:, 0] for v in (h_blocks, p1_blocks, p_blocks)]
    masks = [v[:, 0].T for v in (h_mask, p1_mask, p_mask)]
    return tuple(v[:, None] for v in exchange(values, masks))


def solution(mesh):
    blocks = P(None, "row", "col", None, None)
    masks = P(None, "row", "col")
    return jax.shard_map(
        per_device, mesh=mesh, in_specs=(blocks,) * 3 + (masks,) * 3,
        out_specs=(blocks, blocks), check_vma=False,
    )
```

```python
import functools

import jax
import jax.numpy as jnp
from jax import lax
from jax.experimental import pallas as pl
from jax.experimental.pallas import tpu as pltpu
from jax.sharding import PartitionSpec as P

MESH = pl.DeviceIdType.MESH
NX, NY, NZ, NC = 4, 4, 8, 2
NM = 4
M, O = 0, 1
UP_HOPS = (4, 3)
DOWN_HOPS = (3, 4)


def kernel(h_ref, p1_ref, p_ref, h_mask, p1_mask, p_mask, out_c, out_r, raw, strip, left, far, out_f, back, acc,
           z_recv, z_send, l_recv, y_send, c_send, f_send, p_recv, p_send, q_send,
           fy_send, r_send, r_recv, local_sem):
    row, col = lax.axis_index("row"), lax.axis_index("col")
    x, z = row // NZ, row % NZ
    y, k = col // NC, col % NC
    u = col
    low = z <= u
    x_up, x_dn = (x + 1) % NX, (x + NX - 1) % NX
    z_up, z_dn = (z + 1) % NZ, (z + NZ - 1) % NZ
    y_up, y_dn = (y + 1) % NY, (y + NY - 1) % NY

    def dev(x_=x, y_=y, z_=z, k_=k):
        return (x_ * NZ + z_, y_ * NC + k_)

    dev_zu, dev_zd = dev(z_=z_up), dev(z_=z_dn)
    dev_yu, dev_yd = dev(y_=y_up), dev(y_=y_dn)
    dev_xu, dev_xd = dev(x_=x_up), dev(x_=x_dn)
    dev_c = dev(k_=1 - k)

    def remote(src, dst, send, recv, device):
        return pltpu.make_async_remote_copy(
            src_ref=src, dst_ref=dst, send_sem=send, recv_sem=recv,
            device_id=device, device_id_type=MESH)

    loads = [pltpu.make_async_copy(ref, raw.at[i], local_sem.at[i]) for i, ref in enumerate((h_ref, p1_ref, p_ref))]
    for c in loads:
        c.start()
    barrier = pltpu.get_barrier_semaphore()
    for peer in (dev_zu, dev_zd, dev_yu, dev_yd, dev_xu, dev_xd, dev_c):
        pl.semaphore_signal(barrier, inc=1, device_id=peer, device_id_type=MESH)

    slot_m = jnp.where(low, 1, 0)
    slots = (slot_m, 1 - slot_m)
    own = left.at[u]

    def keep_own(kind):
        for i, mask in enumerate((h_mask, p1_mask, p_mask)):
            for m in range(NM):
                keep = jnp.full((128, 128), mask[slots[kind], m].astype(jnp.float32)).astype(jnp.bfloat16)
                block = raw[i, m, slots[kind]] * keep
                left[u, kind, m, i] = block
                if kind == M:
                    strip[z, M, m, i] = block

    for c in loads:
        c.wait()
    keep_own(M)
    pl.semaphore_wait(barrier, 7)

    def z_copy(up, hop, kind, m):
        origin = (z - hop + NZ) % NZ if up else (z + hop) % NZ
        return remote(strip.at[origin, kind, m], strip.at[origin, kind, m], z_send.at[0 if up else 1, hop, kind, m],
                      z_recv.at[origin, kind, m], dev_zu if up else dev_zd)

    def z_arrival(up, hop, kind, m):
        origin = (z - hop + NZ) % NZ if up else (z + hop) % NZ
        return remote(strip.at[origin, kind, m], strip.at[origin, kind, m],
                      z_send.at[0 if up else 1, 0, kind, m], z_recv.at[origin, kind, m], dev_c)

    def z_round(hop, kind, planes=range(NM)):
        for m in planes:
            for up in (True, False):
                limit = (UP_HOPS if up else DOWN_HOPS)[kind]
                if hop <= limit:
                    z_arrival(up, hop, kind, m).wait_recv()
                    if hop < limit:
                        z_copy(up, hop, kind, m).start()

    for m in range(NM):
        z_copy(True, 0, M, m).start()
        z_copy(False, 0, M, m).start()
    keep_own(O)

    dev_f = (jnp.where(low, x_dn, x_up) * NZ + z, col)
    shift_up = jnp.where(x == NX - 1, 1, 0)
    shift_dn = jnp.where(x == 0, NM - 1, 0)
    f_shift = jnp.where(low, shift_dn, shift_up)

    def f_copy(m):
        there = (m + f_shift) % NM
        return remote(own.at[O, m], strip.at[z, O, there], f_send.at[m], z_recv.at[z, O, there], dev_f)

    for m in range(NM):
        f_copy(m).start()

    def l_wait(who, kind):
        remote(left.at[who, kind], left.at[who, kind], c_send.at[0, 0], l_recv.at[who, kind], dev_c).wait_recv()

    def y_copy(slot, up, kind, relay):
        if relay:
            who = (y_dn if up else y_up) * NC + k
            src = left.at[who, kind]
        else:
            who = u
            src = own.at[kind]
        return remote(src, left.at[who, kind], y_send.at[slot], l_recv.at[who, kind], dev_yu if up else dev_yd)

    y_copies = [y_copy(0, True, M, False), y_copy(1, False, O, False),
                y_copy(2, True, O, False), y_copy(3, False, M, False),
                y_copy(4, True, M, True), y_copy(5, False, O, True)]
    for c in y_copies[:4]:
        c.start()

    def c_copy(d, kind):
        who = ((y + d) % NY) * NC + k
        src = own.at[kind] if d == 0 else left.at[who, kind]
        return remote(src, left.at[who, kind], c_send.at[d, kind], l_recv.at[who, kind], dev_c)

    c_copy(0, M).start()
    c_copy(0, O).start()

    def far_wanted(side, who, kind, at):
        if side == 0:
            inside = who >= z if kind == O else who <= 2 * at + 1
            return jnp.logical_and(2 * at + 1 >= z, inside)
        inside = who < z if kind == O else who > 2 * at
        return jnp.logical_and(2 * at < z, inside)

    def far_by_x(side, d, kind):
        home = (y + d) % NY
        who = home * NC + k
        wanted = far_wanted(side, who, kind, y)
        if d in (1, 3):
            wanted = jnp.logical_and(wanted, jnp.logical_not(far_wanted(side, who, kind, home)))
        return wanted

    def far_sends(d, kind, act):
        who = ((y + d) % NY) * NC + k
        src = own.at[kind] if d == 0 else left.at[who, kind]
        for side in (0, 1):
            @pl.when(far_by_x(side, d, kind))
            def _():
                shift = shift_dn if side == 0 else shift_up
                for m in range(NM):
                    act(remote(src.at[m], far.at[side, who, kind, (m + shift) % NM],
                               p_send.at[side, d, kind, m], p_recv.at[side, who, kind],
                               dev_xd if side == 0 else dev_xu))

    def far_y(kind, act):
        for side in (0, 1):
            for way, (there, device) in enumerate(((y_up, dev_yu), (y_dn, dev_yd))):
                @pl.when(jnp.logical_and(far_wanted(side, u, kind, y), far_wanted(side, u, kind, there)))
                def _():
                    src = strip.at[z, O] if kind == O else far.at[side, u, M]
                    act(remote(src, far.at[side, u, kind], fy_send.at[side, way, kind],
                               p_recv.at[side, u, kind], device))

    def far_pass(d, kind):
        who = ((y + d) % NY) * NC + k
        for side in (0, 1):
            @pl.when(far_wanted(side, who, kind, y))
            def _():
                spot = far.at[side, who, kind]
                remote(spot, spot, q_send.at[side, d, kind], p_recv.at[side, who, kind], dev_c).wait_recv()
                remote(spot, spot, q_send.at[side, d, kind], p_recv.at[side, who, kind], dev_c).start()

    def start(c):
        c.start()

    side_f = jnp.where(low, 0, 1)
    far_sends(0, M, start)

    for m in range(NM):
        acc[m] = jnp.zeros((2, 2, 128, 128), jnp.float32)

    for m in range(NM):
        remote(strip.at[z, O, m], strip.at[z, O, m], f_send.at[m], z_recv.at[z, O, m], dev_c).wait_recv()
        z_copy(True, 0, O, m).start()
        z_copy(False, 0, O, m).start()
    f_keep = pltpu.make_async_copy(strip.at[z, O], far.at[side_f, u, O], local_sem.at[3])
    f_keep.start()
    f_pass = remote(strip.at[z, O], far.at[side_f, u, O], local_sem.at[4], p_recv.at[side_f, u, O], dev_c)
    f_pass.start()

    l_wait(y_dn * NC + k, M)
    y_copies[4].start()
    far_sends(3, M, start)
    c_copy(3, M).start()
    l_wait(y_up * NC + k, O)
    y_copies[5].start()
    far_sends(1, O, start)
    c_copy(1, O).start()
    far_y(O, start)

    z_round(1, M)

    l_wait(y_dn * NC + k, O)
    far_sends(3, O, start)
    c_copy(3, O).start()
    l_wait(y_up * NC + k, M)
    far_sends(1, M, start)
    c_copy(1, M).start()

    far_pass(0, M)
    far_y(M, start)
    z_round(1, O)
    z_round(2, M)

    who2 = ((y + 2) % NY) * NC + k
    l_wait(who2, M)
    far_sends(2, M, start)
    c_copy(2, M).start()
    l_wait(who2, O)
    far_sends(2, O, start)
    c_copy(2, O).start()

    z_round(2, O)
    far_pass(3, O)
    far_pass(1, O)

    zero = jnp.zeros((128, 128), jnp.bfloat16)

    def products(r, m, zp):
        hm, am, pm = (strip[zp, M, m, i] for i in range(3))
        hf, af, pf = (strip[zp, O, m, i] for i in range(3))
        if r == 0:
            ok = jnp.where(zp > u, zp >= z, zp < z)
            first = [left[zp, M, m, i] for i in range(3)]
            second = [jnp.where(ok, left[zp, O, m, i], zero) for i in range(3)]
        else:
            ok_m = jnp.where(low, zp >= z, zp < z)
            ok_f = (zp <= u) == low
            first = [jnp.where(ok_m, far[side_f, zp, O, m, i], zero) for i in range(3)]
            second = [jnp.where(ok_f, far[side_f, zp, M, m, i], zero) for i in range(3)]
        lh, la, lp = (jnp.concatenate([f, s], axis=1) for f, s in zip(first, second))
        one = jnp.dot(jnp.concatenate([lh, lp], axis=0), jnp.concatenate([am, af], axis=0),
                      preferred_element_type=jnp.float32)
        rhs = jnp.concatenate([jnp.concatenate([-hm, pm], axis=1), jnp.concatenate([-hf, pf], axis=1)], axis=0)
        two = jnp.dot(la, rhs, preferred_element_type=jnp.float32)
        return one[:128] + two[:, :128], one[128:] + two[:, 128:]

    def add(r, m, zp):
        c, s = products(r, m, zp)
        acc[m, r, 0] += c
        acc[m, r, 1] += s

    for d in range(NY):
        for kind in (M, O):
            l_wait(((y + d) % NY) * NC + 1 - k, kind)

    def near(i, _):
        add(0, i // 5, (z + i % 5 + 6) % NZ)
        return 0

    lax.fori_loop(0, NM * 5, near, 0)

    z_round(3, M)
    far_pass(3, M)
    far_pass(1, M)
    far_pass(2, M)
    z_round(3, O, (0, 1))
    far_pass(2, O)
    f_keep.wait()
    for d in range(NY):
        who = ((y + d) % NY) * NC + 1 - k
        for kind in (M, O):
            for side in (0, 1):
                @pl.when(far_wanted(side, who, kind, y))
                def _():
                    spot = far.at[side, who, kind]
                    remote(spot, spot, q_send.at[side, d, kind], p_recv.at[side, who, kind], dev_c).wait_recv()

    def far_near(i, _):
        add(1, i // 5, (z + i % 5 + 6) % NZ)
        return 0

    lax.fori_loop(0, 10, far_near, 0)
    z_round(3, O, (2,))
    lax.fori_loop(10, 15, far_near, 0)
    z_round(3, O, (3,))
    lax.fori_loop(15, 20, far_near, 0)

    r_shift = jnp.where(low, shift_up, shift_dn)
    dev_r = (jnp.where(low, x_up, x_dn) * NZ + z, col)

    def r_copy(m):
        there = (m + r_shift) % NM
        return remote(out_f.at[m], back.at[there], r_send.at[m], r_recv.at[there], dev_r)

    def put(m, kind, c, s):
        keep = p1_mask[slots[kind], m].astype(jnp.float32)
        out_c[m, slots[kind]] = (c * keep).astype(jnp.bfloat16)
        out_r[m, slots[kind]] = (s * keep).astype(jnp.bfloat16)

    for m in range(NM):
        def third(i, _):
            add(0, m, (z + 3 + 2 * i) % NZ)
            add(1, m, (z + 3 + 2 * i) % NZ)
            return 0

        lax.fori_loop(0, 2, third, 0)
        z_arrival(True, 4, M, m).wait_recv()
        z_arrival(False, 4, O, m).wait_recv()
        c, s = products(1, m, (z + 4) % NZ)
        out_f[m, 0] = (c + acc[m, 1, 0]).astype(jnp.bfloat16)
        out_f[m, 1] = (s + acc[m, 1, 1]).astype(jnp.bfloat16)
        c, s = products(0, m, (z + 4) % NZ)
        put(m, M, c + acc[m, 0, 0], s + acc[m, 0, 1])
        r_copy(m).start()

    for m in range(NM):
        remote(back.at[m], back.at[m], r_send.at[m], r_recv.at[m], dev_c).wait_recv()
        put(m, O, back[m, 0].astype(jnp.float32), back[m, 1].astype(jnp.float32))

    for m in range(NM):
        r_copy(m).wait_send()
        f_copy(m).wait_send()
        for kind in (M, O):
            for up in (True, False):
                for hop in range((UP_HOPS if up else DOWN_HOPS)[kind]):
                    z_copy(up, hop, kind, m).wait_send()
    for c in y_copies:
        c.wait_send()
    f_pass.wait_send()
    far_y(M, lambda c: c.wait_send())
    far_y(O, lambda c: c.wait_send())
    for d in range(NY):
        who = ((y + d) % NY) * NC + k
        for kind in (M, O):
            c_copy(d, kind).wait_send()
            if (d, kind) != (0, O):
                far_sends(d, kind, lambda c: c.wait_send())
                for side in (0, 1):
                    @pl.when(far_wanted(side, who, kind, y))
                    def _():
                        spot = far.at[side, who, kind]
                        remote(spot, spot, q_send.at[side, d, kind], p_recv.at[side, who, kind], dev_c).wait_send()


def exchange(values, masks):
    dma = pltpu.SemaphoreType.DMA
    block = (128, 128)
    return pl.pallas_call(
        kernel,
        out_shape=(pltpu.VMEM((NM, 2) + block, jnp.bfloat16),) * 2,
        in_specs=[pl.BlockSpec(memory_space=pl.ANY)] * 3 + [pl.BlockSpec(memory_space=pltpu.SMEM)] * 3,
        out_specs=(pl.BlockSpec(memory_space=pltpu.VMEM),) * 2,
        scratch_shapes=[
            pltpu.VMEM((3, NM, 2) + block, jnp.bfloat16),
            pltpu.VMEM((NZ, 2, NM, 3) + block, jnp.bfloat16),
            pltpu.VMEM((8, 2, NM, 3) + block, jnp.bfloat16),
            pltpu.VMEM((2, 8, 2, NM, 3) + block, jnp.bfloat16),
            pltpu.VMEM((NM, 2) + block, jnp.bfloat16),
            pltpu.VMEM((NM, 2) + block, jnp.bfloat16),
            pltpu.VMEM((NM, 2, 2) + block, jnp.float32),
            dma((NZ, 2, NM)),
            dma((2, 4, 2, NM)),
            dma((8, 2)),
            dma((6,)),
            dma((NY, 2)),
            dma((NM,)),
            dma((2, 8, 2)),
            dma((2, NY, 2, NM)),
            dma((2, NY, 2)),
            dma((2, 2, 2)),
            dma((NM,)),
            dma((NM,)),
            dma((5,)),
        ],
        compiler_params=pltpu.CompilerParams(collective_id=0, has_side_effects=True),
        name="exchange",
    )(*values, *masks)


def per_device(h_blocks, p_blocks, p1_blocks, h_mask, p_mask, p1_mask):
    values = [v[:, 0] for v in (h_blocks, p1_blocks, p_blocks)]
    masks = [v[:, 0].T for v in (h_mask, p1_mask, p_mask)]
    return tuple(v[:, None] for v in exchange(values, masks))


def solution(mesh):
    blocks = P(None, "row", "col", None, None)
    masks = P(None, "row", "col")
    return jax.shard_map(
        per_device, mesh=mesh, in_specs=(blocks,) * 3 + (masks,) * 3,
        out_specs=(blocks, blocks), check_vma=False,
    )
```

```python
import functools

import jax
import jax.numpy as jnp
from jax import lax
from jax.experimental import pallas as pl
from jax.experimental.pallas import tpu as pltpu
from jax.sharding import PartitionSpec as P

MESH = pl.DeviceIdType.MESH
NX, NY, NZ, NC = 4, 4, 8, 2
NM = 4
M, O = 0, 1
UP_HOPS = (4, 3)
DOWN_HOPS = (3, 4)


def kernel(h_ref, p1_ref, p_ref, h_mask, p1_mask, p_mask, out_c, out_r, raw, strip, left, far, out_f, back, acc,
           z_recv, z_send, l_recv, y_send, c_send, f_send, p_recv, p_send, q_send,
           fy_send, r_send, r_recv, local_sem):
    row, col = lax.axis_index("row"), lax.axis_index("col")
    x, z = row // NZ, row % NZ
    y, k = col // NC, col % NC
    u = col
    low = z <= u
    x_up, x_dn = (x + 1) % NX, (x + NX - 1) % NX
    z_up, z_dn = (z + 1) % NZ, (z + NZ - 1) % NZ
    y_up, y_dn = (y + 1) % NY, (y + NY - 1) % NY

    def dev(x_=x, y_=y, z_=z, k_=k):
        return (x_ * NZ + z_, y_ * NC + k_)

    dev_zu, dev_zd = dev(z_=z_up), dev(z_=z_dn)
    dev_yu, dev_yd = dev(y_=y_up), dev(y_=y_dn)
    dev_xu, dev_xd = dev(x_=x_up), dev(x_=x_dn)
    dev_c = dev(k_=1 - k)

    def remote(src, dst, send, recv, device):
        return pltpu.make_async_remote_copy(
            src_ref=src, dst_ref=dst, send_sem=send, recv_sem=recv,
            device_id=device, device_id_type=MESH)

    loads = [pltpu.make_async_copy(ref, raw.at[i], local_sem.at[i]) for i, ref in enumerate((h_ref, p1_ref, p_ref))]
    for c in loads:
        c.start()
    barrier = pltpu.get_barrier_semaphore()
    for peer in (dev_zu, dev_zd, dev_yu, dev_yd, dev_xu, dev_xd, dev_c):
        pl.semaphore_signal(barrier, inc=1, device_id=peer, device_id_type=MESH)

    slot_m = jnp.where(low, 1, 0)
    slots = (slot_m, 1 - slot_m)
    own = left.at[u]

    def keep_own(kind):
        for i, mask in enumerate((h_mask, p1_mask, p_mask)):
            for m in range(NM):
                keep = jnp.full((128, 128), mask[slots[kind], m].astype(jnp.float32)).astype(jnp.bfloat16)
                block = raw[i, m, slots[kind]] * keep
                left[u, kind, m, i] = block
                if kind == M:
                    strip[z, M, m, i] = block

    for c in loads:
        c.wait()
    keep_own(M)
    pl.semaphore_wait(barrier, 7)

    def z_copy(up, hop, kind, m):
        origin = (z - hop + NZ) % NZ if up else (z + hop) % NZ
        return remote(strip.at[origin, kind, m], strip.at[origin, kind, m], z_send.at[0 if up else 1, hop, kind, m],
                      z_recv.at[origin, kind, m], dev_zu if up else dev_zd)

    def z_arrival(up, hop, kind, m):
        origin = (z - hop + NZ) % NZ if up else (z + hop) % NZ
        return remote(strip.at[origin, kind, m], strip.at[origin, kind, m],
                      z_send.at[0 if up else 1, 0, kind, m], z_recv.at[origin, kind, m], dev_c)

    def z_round(hop, kind, planes=range(NM)):
        for m in planes:
            for up in (True, False):
                limit = (UP_HOPS if up else DOWN_HOPS)[kind]
                if hop <= limit:
                    z_arrival(up, hop, kind, m).wait_recv()
                    if hop < limit:
                        z_copy(up, hop, kind, m).start()

    for m in range(NM):
        z_copy(True, 0, M, m).start()
        z_copy(False, 0, M, m).start()
    keep_own(O)

    dev_f = (jnp.where(low, x_dn, x_up) * NZ + z, col)
    shift_up = jnp.where(x == NX - 1, 1, 0)
    shift_dn = jnp.where(x == 0, NM - 1, 0)
    f_shift = jnp.where(low, shift_dn, shift_up)

    def f_copy(there):
        m = (there + NM - f_shift) % NM
        return remote(own.at[O, m], strip.at[z, O, there], f_send.at[there], z_recv.at[z, O, there], dev_f)

    for m in range(NM):
        f_copy(m).start()

    def l_wait(who, kind):
        remote(left.at[who, kind], left.at[who, kind], c_send.at[0, 0], l_recv.at[who, kind], dev_c).wait_recv()

    def y_copy(slot, up, kind, relay):
        if relay:
            who = (y_dn if up else y_up) * NC + k
            src = left.at[who, kind]
        else:
            who = u
            src = own.at[kind]
        return remote(src, left.at[who, kind], y_send.at[slot], l_recv.at[who, kind], dev_yu if up else dev_yd)

    y_copies = [y_copy(0, True, M, False), y_copy(1, False, O, False),
                y_copy(2, True, O, False), y_copy(3, False, M, False),
                y_copy(4, True, M, True), y_copy(5, False, O, True)]
    for c in y_copies[:4]:
        c.start()

    def c_copy(d, kind):
        who = ((y + d) % NY) * NC + k
        src = own.at[kind] if d == 0 else left.at[who, kind]
        return remote(src, left.at[who, kind], c_send.at[d, kind], l_recv.at[who, kind], dev_c)

    c_copy(0, M).start()
    c_copy(0, O).start()

    def far_wanted(side, who, kind, at):
        if side == 0:
            inside = who >= z if kind == O else who <= 2 * at + 1
            return jnp.logical_and(2 * at + 1 >= z, inside)
        inside = who < z if kind == O else who > 2 * at
        return jnp.logical_and(2 * at < z, inside)

    def far_by_x(side, d, kind):
        home = (y + d) % NY
        who = home * NC + k
        wanted = far_wanted(side, who, kind, y)
        if d in (1, 3):
            wanted = jnp.logical_and(wanted, jnp.logical_not(far_wanted(side, who, kind, home)))
        return wanted

    def far_sends(d, kind, act):
        who = ((y + d) % NY) * NC + k
        src = own.at[kind] if d == 0 else left.at[who, kind]
        for side in (0, 1):
            @pl.when(far_by_x(side, d, kind))
            def _():
                shift = shift_dn if side == 0 else shift_up
                for m in range(NM):
                    act(remote(src.at[m], far.at[side, who, kind, (m + shift) % NM],
                               p_send.at[side, d, kind, m], p_recv.at[side, who, kind],
                               dev_xd if side == 0 else dev_xu))

    def far_y(kind, act):
        for side in (0, 1):
            for way, (there, device) in enumerate(((y_up, dev_yu), (y_dn, dev_yd))):
                @pl.when(jnp.logical_and(far_wanted(side, u, kind, y), far_wanted(side, u, kind, there)))
                def _():
                    src = strip.at[z, O] if kind == O else far.at[side, u, M]
                    act(remote(src, far.at[side, u, kind], fy_send.at[side, way, kind],
                               p_recv.at[side, u, kind], device))

    def far_pass(d, kind):
        who = ((y + d) % NY) * NC + k
        for side in (0, 1):
            @pl.when(far_wanted(side, who, kind, y))
            def _():
                spot = far.at[side, who, kind]
                remote(spot, spot, q_send.at[side, d, kind], p_recv.at[side, who, kind], dev_c).wait_recv()
                remote(spot, spot, q_send.at[side, d, kind], p_recv.at[side, who, kind], dev_c).start()

    def start(c):
        c.start()

    side_f = jnp.where(low, 0, 1)
    far_sends(0, M, start)

    for m in range(NM):
        acc[m] = jnp.zeros((2, 2, 128, 128), jnp.float32)

    for m in range(NM):
        remote(strip.at[z, O, m], strip.at[z, O, m], f_send.at[m], z_recv.at[z, O, m], dev_c).wait_recv()
        z_copy(True, 0, O, m).start()
        z_copy(False, 0, O, m).start()
    f_keep = pltpu.make_async_copy(strip.at[z, O], far.at[side_f, u, O], local_sem.at[3])
    f_keep.start()
    f_pass = remote(strip.at[z, O], far.at[side_f, u, O], local_sem.at[4], p_recv.at[side_f, u, O], dev_c)
    f_pass.start()

    l_wait(y_dn * NC + k, M)
    y_copies[4].start()
    far_sends(3, M, start)
    c_copy(3, M).start()
    l_wait(y_up * NC + k, O)
    y_copies[5].start()
    far_sends(1, O, start)
    c_copy(1, O).start()
    far_y(O, start)

    z_round(1, M)

    l_wait(y_dn * NC + k, O)
    far_sends(3, O, start)
    c_copy(3, O).start()
    l_wait(y_up * NC + k, M)
    far_sends(1, M, start)
    c_copy(1, M).start()

    far_pass(0, M)
    far_y(M, start)
    z_round(1, O)
    z_round(2, M)

    who2 = ((y + 2) % NY) * NC + k
    l_wait(who2, M)
    far_sends(2, M, start)
    c_copy(2, M).start()
    l_wait(who2, O)
    far_sends(2, O, start)
    c_copy(2, O).start()

    z_round(2, O)
    far_pass(3, O)
    far_pass(1, O)

    zero = jnp.zeros((128, 128), jnp.bfloat16)

    def products(r, m, zp):
        hm, am, pm = (strip[zp, M, m, i] for i in range(3))
        hf, af, pf = (strip[zp, O, m, i] for i in range(3))
        if r == 0:
            ok = jnp.where(zp > u, zp >= z, zp < z)
            first = [left[zp, M, m, i] for i in range(3)]
            second = [jnp.where(ok, left[zp, O, m, i], zero) for i in range(3)]
        else:
            ok_m = jnp.where(low, zp >= z, zp < z)
            ok_f = (zp <= u) == low
            first = [jnp.where(ok_m, far[side_f, zp, O, m, i], zero) for i in range(3)]
            second = [jnp.where(ok_f, far[side_f, zp, M, m, i], zero) for i in range(3)]
        lh, la, lp = (jnp.concatenate([f, s], axis=1) for f, s in zip(first, second))
        one = jnp.dot(jnp.concatenate([lh, lp], axis=0), jnp.concatenate([am, af], axis=0),
                      preferred_element_type=jnp.float32)
        rhs = jnp.concatenate([jnp.concatenate([-hm, pm], axis=1), jnp.concatenate([-hf, pf], axis=1)], axis=0)
        two = jnp.dot(la, rhs, preferred_element_type=jnp.float32)
        return one[:128] + two[:, :128], one[128:] + two[:, 128:]

    def add(r, m, zp):
        c, s = products(r, m, zp)
        acc[m, r, 0] += c
        acc[m, r, 1] += s

    for d in range(NY):
        for kind in (M, O):
            l_wait(((y + d) % NY) * NC + 1 - k, kind)

    def near(i, _):
        add(0, i // 5, (z + i % 5 + 6) % NZ)
        return 0

    lax.fori_loop(0, NM * 5, near, 0)

    z_round(3, M)
    far_pass(3, M)
    far_pass(1, M)
    far_pass(2, M)
    z_round(3, O, (0, 1))
    far_pass(2, O)
    f_keep.wait()
    for d in range(NY):
        who = ((y + d) % NY) * NC + 1 - k
        for kind in (M, O):
            for side in (0, 1):
                @pl.when(far_wanted(side, who, kind, y))
                def _():
                    spot = far.at[side, who, kind]
                    remote(spot, spot, q_send.at[side, d, kind], p_recv.at[side, who, kind], dev_c).wait_recv()

    def far_near(i, _):
        add(1, i // 5, (z + i % 5 + 6) % NZ)
        return 0

    lax.fori_loop(0, 10, far_near, 0)
    z_round(3, O, (2,))
    lax.fori_loop(10, 15, far_near, 0)
    z_round(3, O, (3,))
    lax.fori_loop(15, 20, far_near, 0)

    r_shift = jnp.where(low, shift_up, shift_dn)
    b_shift = jnp.where(low, jnp.where(x == 0, 1, 0), jnp.where(x == NX - 1, NM - 1, 0))
    dev_r = (jnp.where(low, x_up, x_dn) * NZ + z, col)

    def r_copy(m):
        there = (m + r_shift) % NM
        return remote(out_f.at[m], back.at[there], r_send.at[m], r_recv.at[m], dev_r)

    def put(m, kind, c, s):
        keep = p1_mask[slots[kind], m].astype(jnp.float32)
        out_c[m, slots[kind]] = (c * keep).astype(jnp.bfloat16)
        out_r[m, slots[kind]] = (s * keep).astype(jnp.bfloat16)

    for m in range(NM):
        def third(i, _):
            add(0, m, (z + 3 + 2 * i) % NZ)
            add(1, m, (z + 3 + 2 * i) % NZ)
            return 0

        lax.fori_loop(0, 2, third, 0)
        z_arrival(True, 4, M, m).wait_recv()
        z_arrival(False, 4, O, m).wait_recv()
        c, s = products(1, m, (z + 4) % NZ)
        out_f[m, 0] = (c + acc[m, 1, 0]).astype(jnp.bfloat16)
        out_f[m, 1] = (s + acc[m, 1, 1]).astype(jnp.bfloat16)
        c, s = products(0, m, (z + 4) % NZ)
        put(m, M, c + acc[m, 0, 0], s + acc[m, 0, 1])
        r_copy(m).start()

    for sent in range(NM):
        m = (sent + b_shift) % NM
        remote(back.at[m], back.at[m], r_send.at[sent], r_recv.at[sent], dev_c).wait_recv()
        put(m, O, back[m, 0].astype(jnp.float32), back[m, 1].astype(jnp.float32))

    for m in range(NM):
        r_copy(m).wait_send()
        f_copy(m).wait_send()
        for kind in (M, O):
            for up in (True, False):
                for hop in range((UP_HOPS if up else DOWN_HOPS)[kind]):
                    z_copy(up, hop, kind, m).wait_send()
    for c in y_copies:
        c.wait_send()
    f_pass.wait_send()
    far_y(M, lambda c: c.wait_send())
    far_y(O, lambda c: c.wait_send())
    for d in range(NY):
        who = ((y + d) % NY) * NC + k
        for kind in (M, O):
            c_copy(d, kind).wait_send()
            if (d, kind) != (0, O):
                far_sends(d, kind, lambda c: c.wait_send())
                for side in (0, 1):
                    @pl.when(far_wanted(side, who, kind, y))
                    def _():
                        spot = far.at[side, who, kind]
                        remote(spot, spot, q_send.at[side, d, kind], p_recv.at[side, who, kind], dev_c).wait_send()


def exchange(values, masks):
    dma = pltpu.SemaphoreType.DMA
    block = (128, 128)
    return pl.pallas_call(
        kernel,
        out_shape=(pltpu.VMEM((NM, 2) + block, jnp.bfloat16),) * 2,
        in_specs=[pl.BlockSpec(memory_space=pl.ANY)] * 3 + [pl.BlockSpec(memory_space=pltpu.SMEM)] * 3,
        out_specs=(pl.BlockSpec(memory_space=pltpu.VMEM),) * 2,
        scratch_shapes=[
            pltpu.VMEM((3, NM, 2) + block, jnp.bfloat16),
            pltpu.VMEM((NZ, 2, NM, 3) + block, jnp.bfloat16),
            pltpu.VMEM((8, 2, NM, 3) + block, jnp.bfloat16),
            pltpu.VMEM((2, 8, 2, NM, 3) + block, jnp.bfloat16),
            pltpu.VMEM((NM, 2) + block, jnp.bfloat16),
            pltpu.VMEM((NM, 2) + block, jnp.bfloat16),
            pltpu.VMEM((NM, 2, 2) + block, jnp.float32),
            dma((NZ, 2, NM)),
            dma((2, 4, 2, NM)),
            dma((8, 2)),
            dma((6,)),
            dma((NY, 2)),
            dma((NM,)),
            dma((2, 8, 2)),
            dma((2, NY, 2, NM)),
            dma((2, NY, 2)),
            dma((2, 2, 2)),
            dma((NM,)),
            dma((NM,)),
            dma((5,)),
        ],
        compiler_params=pltpu.CompilerParams(collective_id=0, has_side_effects=True),
        name="exchange",
    )(*values, *masks)


def write_out(c_ref, r_ref, oc, orr, sem):
    a = pltpu.make_async_copy(c_ref, oc, sem.at[0])
    b = pltpu.make_async_copy(r_ref, orr, sem.at[1])
    a.start()
    b.start()
    a.wait()
    b.wait()


def finish(c, r):
    c = pltpu.with_memory_space_constraint(c, pltpu.VMEM)
    r = pltpu.with_memory_space_constraint(r, pltpu.VMEM)
    return pl.pallas_call(
        write_out,
        out_shape=(jax.ShapeDtypeStruct(c.shape, c.dtype),) * 2,
        in_specs=[pl.BlockSpec(memory_space=pltpu.VMEM)] * 2,
        out_specs=(pl.BlockSpec(memory_space=pl.ANY),) * 2,
        scratch_shapes=[pltpu.SemaphoreType.DMA((2,))],
        name="finish",
    )(c, r)


def per_device(h_blocks, p_blocks, p1_blocks, h_mask, p_mask, p1_mask):
    values = [v[:, 0] for v in (h_blocks, p1_blocks, p_blocks)]
    masks = [v[:, 0].T for v in (h_mask, p1_mask, p_mask)]
    return tuple(v[:, None] for v in finish(*exchange(values, masks)))


def solution(mesh):
    blocks = P(None, "row", "col", None, None)
    masks = P(None, "row", "col")
    return jax.shard_map(
        per_device, mesh=mesh, in_specs=(blocks,) * 3 + (masks,) * 3,
        out_specs=(blocks, blocks), check_vma=False,
    )
```

```python
import functools

import jax
import jax.numpy as jnp
from jax import lax
from jax.experimental import pallas as pl
from jax.experimental.pallas import tpu as pltpu
from jax.sharding import PartitionSpec as P

MESH = pl.DeviceIdType.MESH
NX, NY, NZ, NC = 4, 4, 8, 2
NM = 4
M, O = 0, 1
UP_HOPS = (4, 3)
DOWN_HOPS = (3, 4)


FINE = ((False, 3, O), (True, 4, M), (False, 4, O))
WHOLE = tuple((up, hop, kind) for up in (True, False) for kind in (M, O)
              for hop in range(1, (UP_HOPS if up else DOWN_HOPS)[kind] + 1) if (up, hop, kind) not in FINE)


def kernel(h_ref, p1_ref, p_ref, h_hbm, p1_hbm, p_hbm, out_c, out_r,
           masks, raw, strip, left, far, out_f, back, acc,
           whole_recv, fine_recv, f_recv, l_recv, c_recv, p_recv, r_recv,
           z_send, y_send, c_send, f_send, p_send, q_send, fy_send, r_send, local_sem):
    row, col = lax.axis_index("row"), lax.axis_index("col")
    x, z = row // NZ, row % NZ
    y, k = col // NC, col % NC
    u = col
    low = z <= u
    x_up, x_dn = (x + 1) % NX, (x + NX - 1) % NX
    z_up, z_dn = (z + 1) % NZ, (z + NZ - 1) % NZ
    y_up, y_dn = (y + 1) % NY, (y + NY - 1) % NY

    def dev(x_=x, y_=y, z_=z, k_=k):
        return (x_ * NZ + z_, y_ * NC + k_)

    dev_zu, dev_zd = dev(z_=z_up), dev(z_=z_dn)
    dev_yu, dev_yd = dev(y_=y_up), dev(y_=y_dn)
    dev_xu, dev_xd = dev(x_=x_up), dev(x_=x_dn)
    dev_c = dev(k_=1 - k)

    def remote(src, dst, send, recv, device):
        return pltpu.make_async_remote_copy(
            src_ref=src, dst_ref=dst, send_sem=send, recv_sem=recv,
            device_id=device, device_id_type=MESH)

    for i, ref in enumerate((h_ref, p1_ref, p_ref)):
        pltpu.make_async_copy(ref, raw.at[i], local_sem.at[0]).start()
    for i, ref in enumerate((h_hbm, p1_hbm, p_hbm)):
        pltpu.make_async_copy(ref, masks.at[i], local_sem.at[1]).start()
    barrier = pltpu.get_barrier_semaphore()
    for peer in (dev_zu, dev_zd, dev_yu, dev_yd, dev_xu, dev_xd, dev_c):
        pl.semaphore_signal(barrier, inc=1, device_id=peer, device_id_type=MESH)

    slot_m = jnp.where(low, 1, 0)
    slots = (slot_m, 1 - slot_m)
    own = left.at[u]

    def keep_own(kind):
        for i in range(3):
            for m in range(NM):
                keep = jnp.full((128, 128), masks[i, slots[kind], m].astype(jnp.float32)).astype(jnp.bfloat16)
                block = raw[i, m, slots[kind]] * keep
                left[u, kind, m, i] = block
                if kind == M:
                    strip[z, M, m, i] = block

    pltpu.make_async_copy(masks, masks, local_sem.at[1]).wait()
    pltpu.make_async_copy(raw, raw, local_sem.at[0]).wait()
    keep_own(M)
    pl.semaphore_wait(barrier, 7)

    def z_from(up, hop):
        return (z - hop + NZ) % NZ if up else (z + hop) % NZ

    def z_sem(up, hop, kind, m):
        key = (up, hop, kind)
        return fine_recv.at[FINE.index(key), m] if key in FINE else whole_recv.at[WHOLE.index(key)]

    def z_copy(up, hop, kind, m):
        spot = strip.at[z_from(up, hop), kind, m]
        return remote(spot, spot, z_send, z_sem(up, hop + 1, kind, m), dev_zu if up else dev_zd)

    def z_wait(up, hop, kind, m=None):
        spot = strip.at[z_from(up, hop), kind] if m is None else strip.at[z_from(up, hop), kind, m]
        remote(spot, spot, z_send, z_sem(up, hop, kind, m), dev_c).wait_recv()

    def z_round(hop, kind, planes=range(NM)):
        for up in (True, False):
            limit = (UP_HOPS if up else DOWN_HOPS)[kind]
            if hop > limit:
                continue
            onward = hop < limit
            if (up, hop, kind) not in FINE and (0 if onward else NM - 1) in planes:
                z_wait(up, hop, kind)
            for m in planes:
                if (up, hop, kind) in FINE:
                    z_wait(up, hop, kind, m)
                if onward:
                    z_copy(up, hop, kind, m).start()

    for m in range(NM):
        z_copy(True, 0, M, m).start()
        z_copy(False, 0, M, m).start()
    keep_own(O)

    dev_f = (jnp.where(low, x_dn, x_up) * NZ + z, col)
    shift_up = jnp.where(x == NX - 1, 1, 0)
    shift_dn = jnp.where(x == 0, NM - 1, 0)
    f_shift = jnp.where(low, shift_dn, shift_up)

    def f_copy(there):
        m = (there + NM - f_shift) % NM
        return remote(own.at[O, m], strip.at[z, O, there], f_send, f_recv.at[there], dev_f)

    for m in range(NM):
        f_copy(m).start()

    def l_wait(d, kind):
        spot = left.at[((y + d) % NY) * NC + k, kind]
        remote(spot, spot, y_send, l_recv.at[d, kind], dev_c).wait_recv()

    def y_copy(up, kind, relay):
        if relay:
            who = (y_dn if up else y_up) * NC + k
            d = 2
        else:
            who = u
            d = 3 if up else 1
        spot = left.at[who, kind]
        return remote(spot, spot, y_send, l_recv.at[d, kind], dev_yu if up else dev_yd)

    y_relays = [y_copy(True, M, True), y_copy(False, O, True)]
    for up, kind in ((True, M), (False, O), (True, O), (False, M)):
        y_copy(up, kind, False).start()

    def c_copy(d, kind):
        spot = left.at[((y + d) % NY) * NC + k, kind]
        return remote(spot, spot, c_send, c_recv, dev_c)

    c_copy(0, M).start()
    c_copy(0, O).start()

    def far_wanted(side, who, kind, at):
        if side == 0:
            inside = who >= z if kind == O else who <= 2 * at + 1
            return jnp.logical_and(2 * at + 1 >= z, inside)
        inside = who < z if kind == O else who > 2 * at
        return jnp.logical_and(2 * at < z, inside)

    def twin(side, who, kind):
        return jnp.logical_and(who == 2 * y + 1, side == 1 and kind == M)

    def far_recv(side, who, kind):
        return p_recv.at[jnp.where(twin(side, who, kind), 16, kind * 8 + who)]

    def far_send(sems, side, d, kind):
        who = ((y + d) % NY) * NC + k
        return sems.at[jnp.where(twin(side, who, kind), 8, kind * NY + d)]

    def far_by_x(side, d, kind):
        home = (y + d) % NY
        who = home * NC + k
        wanted = far_wanted(side, who, kind, y)
        if d in (1, 3):
            wanted = jnp.logical_and(wanted, jnp.logical_not(far_wanted(side, who, kind, home)))
        return wanted

    def far_sends(d, kind, go=True):
        who = ((y + d) % NY) * NC + k
        src = left.at[who, kind]
        for side in (0, 1):
            @pl.when(far_by_x(side, d, kind))
            def _():
                sems = far_send(p_send, side, d, kind), far_recv(side, who, kind)
                if not go:
                    remote(src, src, *sems, dev_xd).wait_send()
                    return
                shift = shift_dn if side == 0 else shift_up
                for m in range(NM):
                    remote(src.at[m], far.at[side, who, kind, (m + shift) % NM], *sems,
                           dev_xd if side == 0 else dev_xu).start()

    def far_y(kind, act):
        for side in (0, 1):
            for way, (there, device) in enumerate(((y_up, dev_yu), (y_dn, dev_yd))):
                @pl.when(jnp.logical_and(far_wanted(side, u, kind, y), far_wanted(side, u, kind, there)))
                def _():
                    src = strip.at[z, O] if kind == O else far.at[side, u, M]
                    act(remote(src, far.at[side, u, kind], fy_send.at[way, kind],
                               p_recv.at[kind * 8 + u], device))

    def far_pass(d, kind):
        who = ((y + d) % NY) * NC + k
        for side in (0, 1):
            @pl.when(far_wanted(side, who, kind, y))
            def _():
                spot = far.at[side, who, kind]
                copy = remote(spot, spot, far_send(q_send, side, d, kind), far_recv(side, who, kind), dev_c)
                copy.wait_recv()
                copy.start()

    def start(c):
        c.start()

    side_f = jnp.where(low, 0, 1)
    far_sends(0, M)

    for m in range(NM):
        acc[m] = jnp.zeros((2, 2, 128, 128), jnp.float32)

    for m in range(NM):
        remote(strip.at[z, O, m], strip.at[z, O, m], f_send, f_recv.at[m], dev_c).wait_recv()
        z_copy(True, 0, O, m).start()
        z_copy(False, 0, O, m).start()
    f_keep = pltpu.make_async_copy(strip.at[z, O], far.at[side_f, u, O], local_sem.at[2])
    f_keep.start()
    f_pass = remote(strip.at[z, O], far.at[side_f, u, O], local_sem.at[3], p_recv.at[8 + u], dev_c)
    f_pass.start()

    l_wait(3, M)
    y_relays[0].start()
    far_sends(3, M)
    c_copy(3, M).start()
    l_wait(1, O)
    y_relays[1].start()
    far_sends(1, O)
    c_copy(1, O).start()
    far_y(O, start)

    z_round(1, M)

    l_wait(3, O)
    far_sends(3, O)
    c_copy(3, O).start()
    l_wait(1, M)
    far_sends(1, M)
    c_copy(1, M).start()

    far_pass(0, M)
    far_y(M, start)
    z_round(1, O)
    z_round(2, M)

    l_wait(2, M)
    far_sends(2, M)
    c_copy(2, M).start()
    l_wait(2, O)
    far_sends(2, O)
    c_copy(2, O).start()

    z_round(2, O)
    far_pass(3, O)
    far_pass(1, O)

    zero = jnp.zeros((128, 128), jnp.bfloat16)

    def products(r, m, zp):
        hm, am, pm = (strip[zp, M, m, i] for i in range(3))
        hf, af, pf = (strip[zp, O, m, i] for i in range(3))
        if r == 0:
            ok = jnp.where(zp > u, zp >= z, zp < z)
            first = [left[zp, M, m, i] for i in range(3)]
            second = [jnp.where(ok, left[zp, O, m, i], zero) for i in range(3)]
        else:
            ok_m = jnp.where(low, zp >= z, zp < z)
            ok_f = (zp <= u) == low
            first = [jnp.where(ok_m, far[side_f, zp, O, m, i], zero) for i in range(3)]
            second = [jnp.where(ok_f, far[side_f, zp, M, m, i], zero) for i in range(3)]
        lh, la, lp = (jnp.concatenate([f, s], axis=1) for f, s in zip(first, second))
        one = jnp.dot(jnp.concatenate([lh, lp], axis=0), jnp.concatenate([am, af], axis=0),
                      preferred_element_type=jnp.float32)
        rhs = jnp.concatenate([jnp.concatenate([-hm, pm], axis=1), jnp.concatenate([-hf, pf], axis=1)], axis=0)
        two = jnp.dot(la, rhs, preferred_element_type=jnp.float32)
        return one[:128] + two[:, :128], one[128:] + two[:, 128:]

    def add(r, m, zp):
        c, s = products(r, m, zp)
        acc[m, r, 0] += c
        acc[m, r, 1] += s

    halves = left.at[pl.ds(0, NY)]
    remote(halves, halves, c_send, c_recv, dev_c).wait_recv()

    def near(i, _):
        add(0, i // 5, (z + i % 5 + 6) % NZ)
        return 0

    lax.fori_loop(0, NM * 5, near, 0)

    z_round(3, M)
    far_pass(3, M)
    far_pass(1, M)
    far_pass(2, M)
    z_round(3, O, (0, 1))
    far_pass(2, O)
    f_keep.wait()
    for d in range(NY):
        who = ((y + d) % NY) * NC + 1 - k
        for kind in (M, O):
            for side in (0, 1):
                @pl.when(far_wanted(side, who, kind, y))
                def _():
                    spot = far.at[side, who, kind]
                    remote(spot, spot, q_send.at[0], far_recv(side, who, kind), dev_c).wait_recv()

    def far_near(i, _):
        add(1, i // 5, (z + i % 5 + 6) % NZ)
        return 0

    lax.fori_loop(0, 10, far_near, 0)
    z_round(3, O, (2,))
    lax.fori_loop(10, 15, far_near, 0)
    z_round(3, O, (3,))
    lax.fori_loop(15, 20, far_near, 0)

    r_shift = jnp.where(low, shift_up, shift_dn)
    b_shift = jnp.where(low, jnp.where(x == 0, 1, 0), jnp.where(x == NX - 1, NM - 1, 0))
    dev_r = (jnp.where(low, x_up, x_dn) * NZ + z, col)

    def r_copy(m):
        there = (m + r_shift) % NM
        return remote(out_f.at[m], back.at[there], r_send, r_recv.at[m], dev_r)

    def put(m, kind, c, s):
        keep = masks[1, slots[kind], m].astype(jnp.float32)
        out_c[m, slots[kind]] = (c * keep).astype(jnp.bfloat16)
        out_r[m, slots[kind]] = (s * keep).astype(jnp.bfloat16)

    for m in range(NM):
        def third(i, _):
            add(0, m, (z + 3 + 2 * i) % NZ)
            add(1, m, (z + 3 + 2 * i) % NZ)
            return 0

        lax.fori_loop(0, 2, third, 0)
        z_wait(True, 4, M, m)
        z_wait(False, 4, O, m)
        c, s = products(1, m, (z + 4) % NZ)
        out_f[m, 0] = (c + acc[m, 1, 0]).astype(jnp.bfloat16)
        out_f[m, 1] = (s + acc[m, 1, 1]).astype(jnp.bfloat16)
        c, s = products(0, m, (z + 4) % NZ)
        put(m, M, c + acc[m, 0, 0], s + acc[m, 0, 1])
        r_copy(m).start()

    for sent in range(NM):
        m = (sent + b_shift) % NM
        remote(back.at[m], back.at[m], r_send, r_recv.at[sent], dev_c).wait_recv()
        put(m, O, back[m, 0].astype(jnp.float32), back[m, 1].astype(jnp.float32))

    def sent_all(ref, sem):
        remote(ref, ref, sem, r_recv.at[0], dev_c).wait_send()

    sent_all(strip.at[pl.ds(0, NZ - 1)], z_send)
    sent_all(left.at[pl.ds(0, 3)], y_send)
    sent_all(left.at[pl.ds(0, NY)], c_send)
    sent_all(strip.at[0, O], f_send)
    sent_all(out_f, r_send)
    sent_all(strip.at[0, O], local_sem.at[3])
    far_y(M, lambda c: c.wait_send())
    far_y(O, lambda c: c.wait_send())
    for d in range(NY):
        who = ((y + d) % NY) * NC + k
        for kind in (M, O):
            if (d, kind) != (0, O):
                far_sends(d, kind, False)
                for side in (0, 1):
                    @pl.when(far_wanted(side, who, kind, y))
                    def _():
                        sent_all(far.at[side, who, kind], far_send(q_send, side, d, kind))


def exchange(values, masks):
    dma = pltpu.SemaphoreType.DMA
    block = (128, 128)
    return pl.pallas_call(
        kernel,
        out_shape=(pltpu.VMEM((NM, 2) + block, jnp.bfloat16),) * 2,
        in_specs=[pl.BlockSpec(memory_space=pl.ANY)] * 6,
        out_specs=(pl.BlockSpec(memory_space=pltpu.VMEM),) * 2,
        scratch_shapes=[
            pltpu.SMEM((3, 2, NM), jnp.int32),
            pltpu.VMEM((3, NM, 2) + block, jnp.bfloat16),
            pltpu.VMEM((NZ, 2, NM, 3) + block, jnp.bfloat16),
            pltpu.VMEM((8, 2, NM, 3) + block, jnp.bfloat16),
            pltpu.VMEM((2, 8, 2, NM, 3) + block, jnp.bfloat16),
            pltpu.VMEM((NM, 2) + block, jnp.bfloat16),
            pltpu.VMEM((NM, 2) + block, jnp.bfloat16),
            pltpu.VMEM((NM, 2, 2) + block, jnp.float32),
            dma((len(WHOLE),)),
            dma((len(FINE), NM)),
            dma((NM,)),
            dma((NY, 2)),
            dma(()),
            dma((17,)),
            dma((NM,)),
            dma(()),
            dma(()),
            dma(()),
            dma(()),
            dma((9,)),
            dma((9,)),
            dma((2, 2)),
            dma(()),
            dma((4,)),
        ],
        compiler_params=pltpu.CompilerParams(collective_id=0, has_side_effects=True),
        name="exchange",
    )(*values, *masks)


def write_out(c_ref, r_ref, oc, orr, sem):
    a = pltpu.make_async_copy(c_ref, oc, sem.at[0])
    b = pltpu.make_async_copy(r_ref, orr, sem.at[1])
    a.start()
    b.start()
    a.wait()
    b.wait()


def finish(c, r):
    c = pltpu.with_memory_space_constraint(c, pltpu.VMEM)
    r = pltpu.with_memory_space_constraint(r, pltpu.VMEM)
    return pl.pallas_call(
        write_out,
        out_shape=(jax.ShapeDtypeStruct(c.shape, c.dtype),) * 2,
        in_specs=[pl.BlockSpec(memory_space=pltpu.VMEM)] * 2,
        out_specs=(pl.BlockSpec(memory_space=pl.ANY),) * 2,
        scratch_shapes=[pltpu.SemaphoreType.DMA((2,))],
        name="finish",
    )(c, r)


def per_device(h_blocks, p_blocks, p1_blocks, h_mask, p_mask, p1_mask):
    values = [v[:, 0] for v in (h_blocks, p1_blocks, p_blocks)]
    masks = [v[:, 0].T for v in (h_mask, p1_mask, p_mask)]
    return tuple(v[:, None] for v in finish(*exchange(values, masks)))


def solution(mesh):
    blocks = P(None, "row", "col", None, None)
    masks = P(None, "row", "col")
    return jax.shard_map(
        per_device, mesh=mesh, in_specs=(blocks,) * 3 + (masks,) * 3,
        out_specs=(blocks, blocks), check_vma=False,
    )
```

```python
import functools

import jax
import jax.numpy as jnp
from jax import lax
from jax.experimental import pallas as pl
from jax.experimental.pallas import tpu as pltpu
from jax.sharding import PartitionSpec as P

MESH = pl.DeviceIdType.MESH
NX, NY, NZ, NC = 4, 4, 8, 2
NM = 4
M, O = 0, 1
UP_HOPS = (4, 3)
DOWN_HOPS = (3, 4)


FINE = ((False, 3, O), (True, 4, M), (False, 4, O))
LAST = FINE[1:]
WHOLE = tuple((up, hop, kind) for up in (True, False) for kind in (M, O)
              for hop in range(1, (UP_HOPS if up else DOWN_HOPS)[kind] + 1) if (up, hop, kind) not in FINE)


def kernel(h_ref, p1_ref, p_ref, h_hbm, p1_hbm, p_hbm, out_c, out_r,
           masks, raw, strip, left, far, out_f, back, acc,
           whole_recv, fine_recv, last_recv, f_recv, l_recv, c_recv, p_recv, r_recv,
           z_send, y_send, c_send, f_send, p_send, q_send, fy_send, r_send, local_sem):
    row, col = lax.axis_index("row"), lax.axis_index("col")
    x, z = row // NZ, row % NZ
    y, k = col // NC, col % NC
    u = col
    low = z <= u
    x_up, x_dn = (x + 1) % NX, (x + NX - 1) % NX
    z_up, z_dn = (z + 1) % NZ, (z + NZ - 1) % NZ
    y_up, y_dn = (y + 1) % NY, (y + NY - 1) % NY

    def dev(x_=x, y_=y, z_=z, k_=k):
        return (x_ * NZ + z_, y_ * NC + k_)

    dev_zu, dev_zd = dev(z_=z_up), dev(z_=z_dn)
    dev_yu, dev_yd = dev(y_=y_up), dev(y_=y_dn)
    dev_xu, dev_xd = dev(x_=x_up), dev(x_=x_dn)
    dev_c = dev(k_=1 - k)

    def remote(src, dst, send, recv, device):
        return pltpu.make_async_remote_copy(
            src_ref=src, dst_ref=dst, send_sem=send, recv_sem=recv,
            device_id=device, device_id_type=MESH)

    for i, ref in enumerate((h_ref, p1_ref, p_ref)):
        pltpu.make_async_copy(ref, raw.at[i], local_sem.at[0]).start()
    for i, ref in enumerate((h_hbm, p1_hbm, p_hbm)):
        pltpu.make_async_copy(ref, masks.at[i], local_sem.at[1]).start()
    barrier = pltpu.get_barrier_semaphore()
    for peer in (dev_zu, dev_zd, dev_yu, dev_yd, dev_xu, dev_xd, dev_c):
        pl.semaphore_signal(barrier, inc=1, device_id=peer, device_id_type=MESH)

    slot_m = jnp.where(low, 1, 0)
    slots = (slot_m, 1 - slot_m)
    own = left.at[u]

    def keep_own(kind):
        for i in range(3):
            for m in range(NM):
                keep = jnp.full((128, 128), masks[i, slots[kind], m].astype(jnp.float32)).astype(jnp.bfloat16)
                block = raw[i, m, slots[kind]] * keep
                left[u, kind, m, i] = block
                if kind == M:
                    strip[z, M, m, i] = block

    pltpu.make_async_copy(masks, masks, local_sem.at[1]).wait()
    pltpu.make_async_copy(raw, raw, local_sem.at[0]).wait()
    keep_own(M)
    pl.semaphore_wait(barrier, 7)

    def z_from(up, hop):
        return (z - hop + NZ) % NZ if up else (z + hop) % NZ

    def z_sem(up, hop, kind, m):
        key = (up, hop, kind)
        return fine_recv.at[FINE.index(key), m] if key in FINE else whole_recv.at[WHOLE.index(key)]

    def z_copy(up, hop, kind, m):
        spot = strip.at[z_from(up, hop), kind, m]
        return remote(spot, spot, z_send, z_sem(up, hop + 1, kind, m), dev_zu if up else dev_zd)

    def z_wait(up, hop, kind, m=None):
        spot = strip.at[z_from(up, hop), kind] if m is None else strip.at[z_from(up, hop), kind, m]
        remote(spot, spot, z_send, z_sem(up, hop, kind, m), dev_c).wait_recv()

    def z_part(up, part, hop=3):
        kind = M if up else O
        spot = strip.at[z_from(up, hop), kind, NM - 1, pl.ds(2 * part, 2 - part)]
        sem = fine_recv.at[1 if up else 2, NM - 1] if part == 0 else last_recv.at[0 if up else 1]
        return remote(spot, spot, z_send, sem, dev_zu if up else dev_zd)

    def z_round(hop, kind, planes=range(NM)):
        for up in (True, False):
            limit = (UP_HOPS if up else DOWN_HOPS)[kind]
            if hop > limit:
                continue
            onward = hop < limit
            if (up, hop, kind) not in FINE and (0 if onward else NM - 1) in planes:
                z_wait(up, hop, kind)
            for m in planes:
                if (up, hop, kind) in FINE:
                    z_wait(up, hop, kind, m)
                if onward and m == NM - 1 and (up, hop + 1, kind) in LAST:
                    z_part(up, 0).start()
                    z_part(up, 1).start()
                elif onward:
                    z_copy(up, hop, kind, m).start()

    for m in range(NM):
        z_copy(True, 0, M, m).start()
        z_copy(False, 0, M, m).start()
    keep_own(O)

    dev_f = (jnp.where(low, x_dn, x_up) * NZ + z, col)
    shift_up = jnp.where(x == NX - 1, 1, 0)
    shift_dn = jnp.where(x == 0, NM - 1, 0)
    f_shift = jnp.where(low, shift_dn, shift_up)

    def f_copy(there):
        m = (there + NM - f_shift) % NM
        return remote(own.at[O, m], strip.at[z, O, there], f_send, f_recv.at[there], dev_f)

    for m in range(NM):
        f_copy(m).start()

    def l_wait(d, kind):
        spot = left.at[((y + d) % NY) * NC + k, kind]
        remote(spot, spot, y_send, l_recv.at[d, kind], dev_c).wait_recv()

    def y_copy(up, kind, relay):
        if relay:
            who = (y_dn if up else y_up) * NC + k
            d = 2
        else:
            who = u
            d = 3 if up else 1
        spot = left.at[who, kind]
        return remote(spot, spot, y_send, l_recv.at[d, kind], dev_yu if up else dev_yd)

    y_relays = [y_copy(True, M, True), y_copy(False, O, True)]
    for up, kind in ((True, M), (False, O), (True, O), (False, M)):
        y_copy(up, kind, False).start()

    def c_copy(d, kind):
        spot = left.at[((y + d) % NY) * NC + k, kind]
        return remote(spot, spot, c_send, c_recv, dev_c)

    c_copy(0, M).start()
    c_copy(0, O).start()

    def far_wanted(side, who, kind, at):
        if side == 0:
            inside = who >= z if kind == O else who <= 2 * at + 1
            return jnp.logical_and(2 * at + 1 >= z, inside)
        inside = who < z if kind == O else who > 2 * at
        return jnp.logical_and(2 * at < z, inside)

    def twin(side, who, kind):
        return jnp.logical_and(who == 2 * y + 1, side == 1 and kind == M)

    def far_recv(side, who, kind):
        return p_recv.at[jnp.where(twin(side, who, kind), 16, kind * 8 + who)]

    def far_send(sems, side, d, kind):
        who = ((y + d) % NY) * NC + k
        return sems.at[jnp.where(twin(side, who, kind), 8, kind * NY + d)]

    def far_by_x(side, d, kind):
        home = (y + d) % NY
        who = home * NC + k
        wanted = far_wanted(side, who, kind, y)
        if d in (1, 3):
            wanted = jnp.logical_and(wanted, jnp.logical_not(far_wanted(side, who, kind, home)))
        return wanted

    def far_sends(d, kind, go=True):
        who = ((y + d) % NY) * NC + k
        src = left.at[who, kind]
        for side in (0, 1):
            @pl.when(far_by_x(side, d, kind))
            def _():
                sems = far_send(p_send, side, d, kind), far_recv(side, who, kind)
                if not go:
                    remote(src, src, *sems, dev_xd).wait_send()
                    return
                shift = shift_dn if side == 0 else shift_up
                for m in range(NM):
                    remote(src.at[m], far.at[side, who, kind, (m + shift) % NM], *sems,
                           dev_xd if side == 0 else dev_xu).start()

    def far_y(kind, act):
        for side in (0, 1):
            for way, (there, device) in enumerate(((y_up, dev_yu), (y_dn, dev_yd))):
                @pl.when(jnp.logical_and(far_wanted(side, u, kind, y), far_wanted(side, u, kind, there)))
                def _():
                    src = strip.at[z, O] if kind == O else far.at[side, u, M]
                    act(remote(src, far.at[side, u, kind], fy_send.at[way, kind],
                               p_recv.at[kind * 8 + u], device))

    def far_pass(d, kind):
        who = ((y + d) % NY) * NC + k
        for side in (0, 1):
            @pl.when(far_wanted(side, who, kind, y))
            def _():
                spot = far.at[side, who, kind]
                copy = remote(spot, spot, far_send(q_send, side, d, kind), far_recv(side, who, kind), dev_c)
                copy.wait_recv()
                copy.start()

    def start(c):
        c.start()

    side_f = jnp.where(low, 0, 1)
    far_sends(0, M)

    for m in range(NM):
        acc[m] = jnp.zeros((2, 2, 128, 128), jnp.float32)

    for m in range(NM):
        remote(strip.at[z, O, m], strip.at[z, O, m], f_send, f_recv.at[m], dev_c).wait_recv()
        z_copy(True, 0, O, m).start()
        z_copy(False, 0, O, m).start()
    f_keep = pltpu.make_async_copy(strip.at[z, O], far.at[side_f, u, O], local_sem.at[2])
    f_keep.start()
    f_pass = remote(strip.at[z, O], far.at[side_f, u, O], local_sem.at[3], p_recv.at[8 + u], dev_c)
    f_pass.start()

    l_wait(3, M)
    y_relays[0].start()
    far_sends(3, M)
    c_copy(3, M).start()
    l_wait(1, O)
    y_relays[1].start()
    far_sends(1, O)
    c_copy(1, O).start()
    far_y(O, start)

    z_round(1, M)

    l_wait(3, O)
    far_sends(3, O)
    c_copy(3, O).start()
    l_wait(1, M)
    far_sends(1, M)
    c_copy(1, M).start()

    far_pass(0, M)
    far_y(M, start)
    z_round(1, O)
    z_round(2, M)

    l_wait(2, M)
    far_sends(2, M)
    c_copy(2, M).start()
    l_wait(2, O)
    far_sends(2, O)
    c_copy(2, O).start()

    z_round(2, O)
    far_pass(3, O)
    far_pass(1, O)

    zero = jnp.zeros((128, 128), jnp.bfloat16)

    def sides(r, m, zp, which):
        if r == 0:
            ok = jnp.where(zp > u, zp >= z, zp < z)
            first = {i: left[zp, M, m, i] for i in which}
            second = {i: jnp.where(ok, left[zp, O, m, i], zero) for i in which}
        else:
            ok_m = jnp.where(low, zp >= z, zp < z)
            ok_f = (zp <= u) == low
            first = {i: jnp.where(ok_m, far[side_f, zp, O, m, i], zero) for i in which}
            second = {i: jnp.where(ok_f, far[side_f, zp, M, m, i], zero) for i in which}
        return {i: jnp.concatenate([first[i], second[i]], axis=1) for i in which}

    def products(r, m, zp):
        hm, am, pm = (strip[zp, M, m, i] for i in range(3))
        hf, af, pf = (strip[zp, O, m, i] for i in range(3))
        lhs = sides(r, m, zp, (0, 1, 2))
        one = jnp.dot(jnp.concatenate([lhs[0], lhs[2]], axis=0), jnp.concatenate([am, af], axis=0),
                      preferred_element_type=jnp.float32)
        rhs = jnp.concatenate([jnp.concatenate([-hm, pm], axis=1), jnp.concatenate([-hf, pf], axis=1)], axis=0)
        two = jnp.dot(lhs[1], rhs, preferred_element_type=jnp.float32)
        return one[:128] + two[:, :128], one[128:] + two[:, 128:]

    def one_product(r, m, zp, i):
        lhs = sides(r, m, zp, (i, 1))
        bm, am, bf, af = strip[zp, M, m, i], strip[zp, M, m, 1], strip[zp, O, m, i], strip[zp, O, m, 1]
        if i == 0:
            bm, bf = -bm, -bf
        return jnp.dot(jnp.concatenate([lhs[i], lhs[1]], axis=1), jnp.concatenate([am, af, bm, bf], axis=0),
                       preferred_element_type=jnp.float32)

    def add(r, m, zp):
        c, s = products(r, m, zp)
        acc[m, r, 0] += c
        acc[m, r, 1] += s

    halves = left.at[pl.ds(0, NY)]
    remote(halves, halves, c_send, c_recv, dev_c).wait_recv()

    def near(i, _):
        add(0, i // 5, (z + i % 5 + 6) % NZ)
        return 0

    lax.fori_loop(0, NM * 5, near, 0)

    z_round(3, M)
    far_pass(3, M)
    far_pass(1, M)
    far_pass(2, M)
    z_round(3, O, (0, 1))
    far_pass(2, O)
    f_keep.wait()
    for d in range(NY):
        who = ((y + d) % NY) * NC + 1 - k
        for kind in (M, O):
            for side in (0, 1):
                @pl.when(far_wanted(side, who, kind, y))
                def _():
                    spot = far.at[side, who, kind]
                    remote(spot, spot, q_send.at[0], far_recv(side, who, kind), dev_c).wait_recv()

    def far_near(i, _):
        add(1, i // 5, (z + i % 5 + 6) % NZ)
        return 0

    lax.fori_loop(0, 10, far_near, 0)
    z_round(3, O, (2,))
    lax.fori_loop(10, 15, far_near, 0)
    z_round(3, O, (3,))
    lax.fori_loop(15, 20, far_near, 0)

    r_shift = jnp.where(low, shift_up, shift_dn)
    b_shift = jnp.where(low, jnp.where(x == 0, 1, 0), jnp.where(x == NX - 1, NM - 1, 0))
    dev_r = (jnp.where(low, x_up, x_dn) * NZ + z, col)

    def r_copy(m):
        there = (m + r_shift) % NM
        return remote(out_f.at[m], back.at[there], r_send, r_recv.at[m], dev_r)

    def r_part(i):
        there = (NM - 1 + r_shift) % NM
        return remote(out_f.at[NM - 1, i], back.at[there, i], r_send, r_recv.at[NM - 1 + i], dev_r)

    def put(m, kind, c, s):
        keep = masks[1, slots[kind], m].astype(jnp.float32)
        out_c[m, slots[kind]] = (c * keep).astype(jnp.bfloat16)
        out_r[m, slots[kind]] = (s * keep).astype(jnp.bfloat16)

    for m in range(NM):
        def third(i, _):
            add(0, m, (z + 3 + 2 * i) % NZ)
            add(1, m, (z + 3 + 2 * i) % NZ)
            return 0

        lax.fori_loop(0, 2, third, 0)
        opposite = (z + 4) % NZ
        if m < NM - 1:
            z_wait(True, 4, M, m)
            z_wait(False, 4, O, m)
            c, s = products(1, m, opposite)
            out_f[m, 0] = (c + acc[m, 1, 0]).astype(jnp.bfloat16)
            out_f[m, 1] = (s + acc[m, 1, 1]).astype(jnp.bfloat16)
            c, s = products(0, m, opposite)
            put(m, M, c + acc[m, 0, 0], s + acc[m, 0, 1])
            r_copy(m).start()
        else:
            total = []
            for i in range(2):
                for up in (True, False):
                    z_part(up, i, 4).wait_recv()
                out_f[m, i] = (one_product(1, m, opposite, 2 * i) + acc[m, 1, i]).astype(jnp.bfloat16)
                total.append(one_product(0, m, opposite, 2 * i) + acc[m, 0, i])
                r_part(i).start()
            put(m, M, *total)

    for sent in range(NM):
        m = (sent + b_shift) % NM
        if sent < NM - 1:
            remote(back.at[m], back.at[m], r_send, r_recv.at[sent], dev_c).wait_recv()
        else:
            for i in range(2):
                remote(back.at[m, i], back.at[m, i], r_send, r_recv.at[sent + i], dev_c).wait_recv()
        put(m, O, back[m, 0].astype(jnp.float32), back[m, 1].astype(jnp.float32))

    def sent_all(ref, sem):
        remote(ref, ref, sem, r_recv.at[0], dev_c).wait_send()

    sent_all(strip.at[pl.ds(0, NZ - 1)], z_send)
    sent_all(left.at[pl.ds(0, 3)], y_send)
    sent_all(left.at[pl.ds(0, NY)], c_send)
    sent_all(strip.at[0, O], f_send)
    sent_all(out_f, r_send)
    sent_all(strip.at[0, O], local_sem.at[3])
    far_y(M, lambda c: c.wait_send())
    far_y(O, lambda c: c.wait_send())
    for d in range(NY):
        who = ((y + d) % NY) * NC + k
        for kind in (M, O):
            if (d, kind) != (0, O):
                far_sends(d, kind, False)
                for side in (0, 1):
                    @pl.when(far_wanted(side, who, kind, y))
                    def _():
                        sent_all(far.at[side, who, kind], far_send(q_send, side, d, kind))


def exchange(values, masks):
    dma = pltpu.SemaphoreType.DMA
    block = (128, 128)
    return pl.pallas_call(
        kernel,
        out_shape=(pltpu.VMEM((NM, 2) + block, jnp.bfloat16),) * 2,
        in_specs=[pl.BlockSpec(memory_space=pl.ANY)] * 6,
        out_specs=(pl.BlockSpec(memory_space=pltpu.VMEM),) * 2,
        scratch_shapes=[
            pltpu.SMEM((3, 2, NM), jnp.int32),
            pltpu.VMEM((3, NM, 2) + block, jnp.bfloat16),
            pltpu.VMEM((NZ, 2, NM, 3) + block, jnp.bfloat16),
            pltpu.VMEM((8, 2, NM, 3) + block, jnp.bfloat16),
            pltpu.VMEM((2, 8, 2, NM, 3) + block, jnp.bfloat16),
            pltpu.VMEM((NM, 2) + block, jnp.bfloat16),
            pltpu.VMEM((NM, 2) + block, jnp.bfloat16),
            pltpu.VMEM((NM, 2, 2) + block, jnp.float32),
            dma((len(WHOLE),)),
            dma((len(FINE), NM)),
            dma((2,)),
            dma((NM,)),
            dma((NY, 2)),
            dma(()),
            dma((17,)),
            dma((NM + 1,)),
            dma(()),
            dma(()),
            dma(()),
            dma(()),
            dma((9,)),
            dma((9,)),
            dma((2, 2)),
            dma(()),
            dma((4,)),
        ],
        compiler_params=pltpu.CompilerParams(collective_id=0, has_side_effects=True),
        name="exchange",
    )(*values, *masks)


def write_out(c_ref, r_ref, oc, orr, sem):
    a = pltpu.make_async_copy(c_ref, oc, sem.at[0])
    b = pltpu.make_async_copy(r_ref, orr, sem.at[1])
    a.start()
    b.start()
    a.wait()
    b.wait()


def finish(c, r):
    c = pltpu.with_memory_space_constraint(c, pltpu.VMEM)
    r = pltpu.with_memory_space_constraint(r, pltpu.VMEM)
    return pl.pallas_call(
        write_out,
        out_shape=(jax.ShapeDtypeStruct(c.shape, c.dtype),) * 2,
        in_specs=[pl.BlockSpec(memory_space=pltpu.VMEM)] * 2,
        out_specs=(pl.BlockSpec(memory_space=pl.ANY),) * 2,
        scratch_shapes=[pltpu.SemaphoreType.DMA((2,))],
        name="finish",
    )(c, r)


def per_device(h_blocks, p_blocks, p1_blocks, h_mask, p_mask, p1_mask):
    values = [v[:, 0] for v in (h_blocks, p1_blocks, p_blocks)]
    masks = [v[:, 0].T for v in (h_mask, p1_mask, p_mask)]
    return tuple(v[:, None] for v in finish(*exchange(values, masks)))


def solution(mesh):
    blocks = P(None, "row", "col", None, None)
    masks = P(None, "row", "col")
    return jax.shard_map(
        per_device, mesh=mesh, in_specs=(blocks,) * 3 + (masks,) * 3,
        out_specs=(blocks, blocks), check_vma=False,
    )
```

```python
import functools

import jax
import jax.numpy as jnp
from jax import lax
from jax.experimental import pallas as pl
from jax.experimental.pallas import tpu as pltpu
from jax.sharding import PartitionSpec as P

MESH = pl.DeviceIdType.MESH
NX, NY, NZ, NC = 4, 4, 8, 2
NM = 4
M, O = 0, 1
UP_HOPS = (4, 3)
DOWN_HOPS = (3, 4)


FINE = ((False, 3, O), (True, 4, M), (False, 4, O))
LAST = FINE[1:]
WHOLE = tuple((up, hop, kind) for up in (True, False) for kind in (M, O)
              for hop in range(1, (UP_HOPS if up else DOWN_HOPS)[kind] + 1) if (up, hop, kind) not in FINE)


def kernel(h_ref, p1_ref, p_ref, h_hbm, p1_hbm, p_hbm, out_c, out_r,
           masks, raw, strip, left, far, out_f, back, acc,
           whole_recv, fine_recv, last_recv, f_recv, l_recv, c_recv, p_recv, r_recv,
           z_send, y_send, c_send, f_send, p_send, q_send, fy_send, r_send, local_sem):
    row, col = lax.axis_index("row"), lax.axis_index("col")
    x, z = row // NZ, row % NZ
    y, k = col // NC, col % NC
    u = col
    low = z <= u
    x_up, x_dn = (x + 1) % NX, (x + NX - 1) % NX
    z_up, z_dn = (z + 1) % NZ, (z + NZ - 1) % NZ
    y_up, y_dn = (y + 1) % NY, (y + NY - 1) % NY

    def dev(x_=x, y_=y, z_=z, k_=k):
        return (x_ * NZ + z_, y_ * NC + k_)

    dev_zu, dev_zd = dev(z_=z_up), dev(z_=z_dn)
    dev_yu, dev_yd = dev(y_=y_up), dev(y_=y_dn)
    dev_xu, dev_xd = dev(x_=x_up), dev(x_=x_dn)
    dev_c = dev(k_=1 - k)

    def remote(src, dst, send, recv, device):
        return pltpu.make_async_remote_copy(
            src_ref=src, dst_ref=dst, send_sem=send, recv_sem=recv,
            device_id=device, device_id_type=MESH)

    for i, ref in enumerate((h_ref, p1_ref, p_ref)):
        pltpu.make_async_copy(ref, raw.at[i], local_sem.at[0]).start()
    for i, ref in enumerate((h_hbm, p1_hbm, p_hbm)):
        pltpu.make_async_copy(ref, masks.at[i], local_sem.at[1]).start()
    barrier = pltpu.get_barrier_semaphore()
    for peer in (dev_zu, dev_zd, dev_yu, dev_yd, dev_xu, dev_xd, dev_c):
        pl.semaphore_signal(barrier, inc=1, device_id=peer, device_id_type=MESH)

    slot_m = jnp.where(low, 1, 0)
    slots = (slot_m, 1 - slot_m)
    own = left.at[u]

    def keep_own(kind):
        for i in range(3):
            for m in range(NM):
                keep = jnp.full((128, 128), masks[i, slots[kind], m].astype(jnp.float32)).astype(jnp.bfloat16)
                block = raw[i, m, slots[kind]] * keep
                left[u, kind, m, i] = block
                if kind == M:
                    strip[z, M, m, i] = block

    pltpu.make_async_copy(masks, masks, local_sem.at[1]).wait()
    pltpu.make_async_copy(raw, raw, local_sem.at[0]).wait()
    keep_own(M)
    pl.semaphore_wait(barrier, 7)

    def z_from(up, hop):
        return (z - hop + NZ) % NZ if up else (z + hop) % NZ

    def z_sem(up, hop, kind, m):
        key = (up, hop, kind)
        return fine_recv.at[FINE.index(key), m] if key in FINE else whole_recv.at[WHOLE.index(key)]

    def z_copy(up, hop, kind, m):
        spot = strip.at[z_from(up, hop), kind, m]
        return remote(spot, spot, z_send, z_sem(up, hop + 1, kind, m), dev_zu if up else dev_zd)

    def z_wait(up, hop, kind, m=None):
        spot = strip.at[z_from(up, hop), kind] if m is None else strip.at[z_from(up, hop), kind, m]
        remote(spot, spot, z_send, z_sem(up, hop, kind, m), dev_c).wait_recv()

    def z_part(up, part, hop=3):
        kind = M if up else O
        spot = strip.at[z_from(up, hop), kind, NM - 1, pl.ds(2 * part, 2 - part)]
        sem = fine_recv.at[1 if up else 2, NM - 1] if part == 0 else last_recv.at[0 if up else 1]
        return remote(spot, spot, z_send, sem, dev_zu if up else dev_zd)

    def z_round(hop, kind, planes=range(NM)):
        for up in (True, False):
            limit = (UP_HOPS if up else DOWN_HOPS)[kind]
            if hop > limit:
                continue
            onward = hop < limit
            if (up, hop, kind) not in FINE and (0 if onward else NM - 1) in planes:
                z_wait(up, hop, kind)
            for m in planes:
                if (up, hop, kind) in FINE:
                    z_wait(up, hop, kind, m)
                if onward and m == NM - 1 and (up, hop + 1, kind) in LAST:
                    z_part(up, 0).start()
                    z_part(up, 1).start()
                elif onward:
                    z_copy(up, hop, kind, m).start()

    for m in range(NM):
        z_copy(True, 0, M, m).start()
        z_copy(False, 0, M, m).start()
    keep_own(O)

    dev_f = (jnp.where(low, x_dn, x_up) * NZ + z, col)
    shift_up = jnp.where(x == NX - 1, 1, 0)
    shift_dn = jnp.where(x == 0, NM - 1, 0)
    f_shift = jnp.where(low, shift_dn, shift_up)

    def f_copy(there):
        m = (there + NM - f_shift) % NM
        return remote(own.at[O, m], strip.at[z, O, there], f_send, f_recv.at[there], dev_f)

    for m in range(NM):
        f_copy(m).start()

    def l_wait(d, kind):
        spot = left.at[((y + d) % NY) * NC + k, kind]
        remote(spot, spot, y_send, l_recv.at[d - 1, kind], dev_c).wait_recv()

    def y_copy(up, kind, relay):
        if relay:
            who = (y_dn if up else y_up) * NC + k
            d = 2
        else:
            who = u
            d = 3 if up else 1
        spot = left.at[who, kind]
        return remote(spot, spot, y_send, l_recv.at[d - 1, kind], dev_yu if up else dev_yd)

    y_relays = [y_copy(True, M, True), y_copy(False, O, True)]
    for up, kind in ((True, M), (False, O), (True, O), (False, M)):
        y_copy(up, kind, False).start()

    def c_copy(d, kind):
        spot = left.at[((y + d) % NY) * NC + k, kind]
        return remote(spot, spot, c_send, c_recv, dev_c)

    c_copy(0, M).start()
    c_copy(0, O).start()

    def far_wanted(side, who, kind, at):
        if side == 0:
            inside = who >= z if kind == O else who <= 2 * at + 1
            return jnp.logical_and(2 * at + 1 >= z, inside)
        inside = who < z if kind == O else who > 2 * at
        return jnp.logical_and(2 * at < z, inside)

    def twin(side, who, kind):
        return jnp.logical_and(who == 2 * y + 1, side == 1 and kind == M)

    def far_recv(side, who, kind):
        return p_recv.at[jnp.where(twin(side, who, kind), 16, kind * 8 + who)]

    def far_send(sems, side, d, kind):
        who = ((y + d) % NY) * NC + k
        return sems.at[jnp.where(twin(side, who, kind), 8, kind * NY + d)]

    def far_by_x(side, d, kind):
        home = (y + d) % NY
        who = home * NC + k
        wanted = far_wanted(side, who, kind, y)
        if d in (1, 3):
            wanted = jnp.logical_and(wanted, jnp.logical_not(far_wanted(side, who, kind, home)))
        return wanted

    def far_sends(d, kind, go=True):
        who = ((y + d) % NY) * NC + k
        src = left.at[who, kind]
        for side in (0, 1):
            @pl.when(far_by_x(side, d, kind))
            def _():
                sems = far_send(p_send, side, d, kind), far_recv(side, who, kind)
                if not go:
                    remote(src, src, *sems, dev_xd).wait_send()
                    return
                shift = shift_dn if side == 0 else shift_up
                for m in range(NM):
                    remote(src.at[m], far.at[side, who, kind, (m + shift) % NM], *sems,
                           dev_xd if side == 0 else dev_xu).start()

    def far_y(kind, act):
        for side in (0, 1):
            for way, (there, device) in enumerate(((y_up, dev_yu), (y_dn, dev_yd))):
                @pl.when(jnp.logical_and(far_wanted(side, u, kind, y), far_wanted(side, u, kind, there)))
                def _():
                    src = strip.at[z, O] if kind == O else far.at[side, u, M]
                    act(remote(src, far.at[side, u, kind], fy_send.at[way, kind],
                               p_recv.at[kind * 8 + u], device))

    def far_pass(d, kind):
        who = ((y + d) % NY) * NC + k
        for side in (0, 1):
            @pl.when(far_wanted(side, who, kind, y))
            def _():
                spot = far.at[side, who, kind]
                copy = remote(spot, spot, far_send(q_send, side, d, kind), far_recv(side, who, kind), dev_c)
                copy.wait_recv()
                copy.start()

    def start(c):
        c.start()

    side_f = jnp.where(low, 0, 1)
    far_sends(0, M)

    for m in range(NM):
        acc[m] = jnp.zeros((2, 2, 128, 128), jnp.float32)

    for m in range(NM):
        remote(strip.at[z, O, m], strip.at[z, O, m], f_send, f_recv.at[m], dev_c).wait_recv()
        z_copy(True, 0, O, m).start()
        z_copy(False, 0, O, m).start()
    f_keep = pltpu.make_async_copy(strip.at[z, O], far.at[side_f, u, O], local_sem.at[2])
    f_keep.start()
    f_pass = remote(strip.at[z, O], far.at[side_f, u, O], local_sem.at[3], p_recv.at[8 + u], dev_c)
    f_pass.start()

    l_wait(3, M)
    y_relays[0].start()
    far_sends(3, M)
    c_copy(3, M).start()
    l_wait(1, O)
    y_relays[1].start()
    far_sends(1, O)
    c_copy(1, O).start()
    far_y(O, start)

    z_round(1, M)

    l_wait(3, O)
    far_sends(3, O)
    c_copy(3, O).start()
    l_wait(1, M)
    far_sends(1, M)
    c_copy(1, M).start()

    far_pass(0, M)
    far_y(M, start)
    z_round(1, O)
    z_round(2, M)

    l_wait(2, M)
    far_sends(2, M)
    c_copy(2, M).start()
    l_wait(2, O)
    far_sends(2, O)
    c_copy(2, O).start()

    z_round(2, O)
    far_pass(3, O)
    far_pass(1, O)

    zero = jnp.zeros((128, 128), jnp.bfloat16)

    def sides(r, m, zp, which):
        if r == 0:
            ok = jnp.where(zp > u, zp >= z, zp < z)
            first = {i: left[zp, M, m, i] for i in which}
            second = {i: jnp.where(ok, left[zp, O, m, i], zero) for i in which}
        else:
            ok_m = jnp.where(low, zp >= z, zp < z)
            ok_f = (zp <= u) == low
            first = {i: jnp.where(ok_m, far[side_f, zp, O, m, i], zero) for i in which}
            second = {i: jnp.where(ok_f, far[side_f, zp, M, m, i], zero) for i in which}
        return {i: jnp.concatenate([first[i], second[i]], axis=1) for i in which}

    def products(r, m, zp):
        hm, am, pm = (strip[zp, M, m, i] for i in range(3))
        hf, af, pf = (strip[zp, O, m, i] for i in range(3))
        lhs = sides(r, m, zp, (0, 1, 2))
        one = jnp.dot(jnp.concatenate([lhs[0], lhs[2]], axis=0), jnp.concatenate([am, af], axis=0),
                      preferred_element_type=jnp.float32)
        rhs = jnp.concatenate([jnp.concatenate([-hm, pm], axis=1), jnp.concatenate([-hf, pf], axis=1)], axis=0)
        two = jnp.dot(lhs[1], rhs, preferred_element_type=jnp.float32)
        return one[:128] + two[:, :128], one[128:] + two[:, 128:]

    def one_product(r, m, zp, i):
        lhs = sides(r, m, zp, (i, 1))
        bm, am, bf, af = strip[zp, M, m, i], strip[zp, M, m, 1], strip[zp, O, m, i], strip[zp, O, m, 1]
        if i == 0:
            bm, bf = -bm, -bf
        return jnp.dot(jnp.concatenate([lhs[i], lhs[1]], axis=1), jnp.concatenate([am, af, bm, bf], axis=0),
                       preferred_element_type=jnp.float32)

    def add(r, m, zp):
        c, s = products(r, m, zp)
        acc[m, r, 0] += c
        acc[m, r, 1] += s

    halves = left.at[pl.ds(0, NY)]
    remote(halves, halves, c_send, c_recv, dev_c).wait_recv()

    def near(i, _):
        add(0, i // 5, (z + i % 5 + 6) % NZ)
        return 0

    lax.fori_loop(0, NM * 5, near, 0)

    z_round(3, M)
    far_pass(3, M)
    far_pass(1, M)
    far_pass(2, M)
    z_round(3, O, (0, 1))
    far_pass(2, O)
    f_keep.wait()
    for d in range(NY):
        who = ((y + d) % NY) * NC + 1 - k
        for kind in (M, O):
            for side in (0, 1):
                @pl.when(far_wanted(side, who, kind, y))
                def _():
                    spot = far.at[side, who, kind]
                    remote(spot, spot, q_send.at[0], far_recv(side, who, kind), dev_c).wait_recv()

    def far_near(i, _):
        add(1, i // 5, (z + i % 5 + 6) % NZ)
        return 0

    lax.fori_loop(0, 10, far_near, 0)
    z_round(3, O, (2,))
    lax.fori_loop(10, 15, far_near, 0)
    z_round(3, O, (3,))
    lax.fori_loop(15, 20, far_near, 0)

    r_shift = jnp.where(low, shift_up, shift_dn)
    b_shift = jnp.where(low, jnp.where(x == 0, 1, 0), jnp.where(x == NX - 1, NM - 1, 0))
    dev_r = (jnp.where(low, x_up, x_dn) * NZ + z, col)

    def r_copy(m):
        there = (m + r_shift) % NM
        return remote(out_f.at[m], back.at[there], r_send, r_recv.at[m], dev_r)

    def r_part(i):
        there = (NM - 1 + r_shift) % NM
        return remote(out_f.at[NM - 1, i], back.at[there, i], r_send, r_recv.at[NM - 1 + i], dev_r)

    def put(m, kind, c, s):
        keep = masks[1, slots[kind], m].astype(jnp.float32)
        out_c[m, slots[kind]] = (c * keep).astype(jnp.bfloat16)
        out_r[m, slots[kind]] = (s * keep).astype(jnp.bfloat16)

    for m in range(NM):
        def third(i, _):
            add(0, m, (z + 3 + 2 * i) % NZ)
            add(1, m, (z + 3 + 2 * i) % NZ)
            return 0

        lax.fori_loop(0, 2, third, 0)
        opposite = (z + 4) % NZ
        if m < NM - 1:
            z_wait(True, 4, M, m)
            z_wait(False, 4, O, m)
            c, s = products(1, m, opposite)
            out_f[m, 0] = (c + acc[m, 1, 0]).astype(jnp.bfloat16)
            out_f[m, 1] = (s + acc[m, 1, 1]).astype(jnp.bfloat16)
            c, s = products(0, m, opposite)
            put(m, M, c + acc[m, 0, 0], s + acc[m, 0, 1])
            r_copy(m).start()
        else:
            total = []
            for i in range(2):
                for up in (True, False):
                    z_part(up, i, 4).wait_recv()
                out_f[m, i] = (one_product(1, m, opposite, 2 * i) + acc[m, 1, i]).astype(jnp.bfloat16)
                total.append(one_product(0, m, opposite, 2 * i) + acc[m, 0, i])
                r_part(i).start()
            put(m, M, *total)

    def sent_all(ref, sem):
        remote(ref, ref, sem, r_recv.at[0], dev_c).wait_send()

    sent_all(strip.at[pl.ds(0, NZ - 1)], z_send)
    sent_all(left.at[pl.ds(0, 3)], y_send)
    sent_all(left.at[pl.ds(0, NY)], c_send)
    sent_all(strip.at[0, O], f_send)
    sent_all(strip.at[0, O], local_sem.at[3])
    far_y(M, lambda c: c.wait_send())
    far_y(O, lambda c: c.wait_send())
    for d in range(NY):
        who = ((y + d) % NY) * NC + k
        for kind in (M, O):
            if (d, kind) != (0, O):
                far_sends(d, kind, False)
                for side in (0, 1):
                    @pl.when(far_wanted(side, who, kind, y))
                    def _():
                        sent_all(far.at[side, who, kind], far_send(q_send, side, d, kind))

    for sent in range(NM):
        m = (sent + b_shift) % NM
        if sent < NM - 1:
            remote(back.at[m], back.at[m], r_send, r_recv.at[sent], dev_c).wait_recv()
        else:
            for i in range(2):
                remote(back.at[m, i], back.at[m, i], r_send, r_recv.at[sent + i], dev_c).wait_recv()
        put(m, O, back[m, 0].astype(jnp.float32), back[m, 1].astype(jnp.float32))
    sent_all(out_f, r_send)


def exchange(values, masks):
    dma = pltpu.SemaphoreType.DMA
    block = (128, 128)
    return pl.pallas_call(
        kernel,
        out_shape=(pltpu.VMEM((NM, 2) + block, jnp.bfloat16),) * 2,
        in_specs=[pl.BlockSpec(memory_space=pl.ANY)] * 6,
        out_specs=(pl.BlockSpec(memory_space=pltpu.VMEM),) * 2,
        scratch_shapes=[
            pltpu.SMEM((3, 2, NM), jnp.int32),
            pltpu.VMEM((3, NM, 2) + block, jnp.bfloat16),
            pltpu.VMEM((NZ, 2, NM, 3) + block, jnp.bfloat16),
            pltpu.VMEM((8, 2, NM, 3) + block, jnp.bfloat16),
            pltpu.VMEM((2, 8, 2, NM, 3) + block, jnp.bfloat16),
            pltpu.VMEM((NM, 2) + block, jnp.bfloat16),
            pltpu.VMEM((NM, 2) + block, jnp.bfloat16),
            pltpu.VMEM((NM, 2, 2) + block, jnp.float32),
            dma((len(WHOLE),)),
            dma((len(FINE), NM)),
            dma((2,)),
            dma((NM,)),
            dma((NY - 1, 2)),
            dma(()),
            dma((17,)),
            dma((NM + 1,)),
            dma(()),
            dma(()),
            dma(()),
            dma(()),
            dma((9,)),
            dma((9,)),
            dma((2, 2)),
            dma(()),
            dma((4,)),
        ],
        compiler_params=pltpu.CompilerParams(collective_id=0, has_side_effects=True),
        name="exchange",
    )(*values, *masks)


def write_out(c_ref, r_ref, oc, orr, sem):
    a = pltpu.make_async_copy(c_ref, oc, sem.at[0])
    b = pltpu.make_async_copy(r_ref, orr, sem.at[1])
    a.start()
    b.start()
    a.wait()
    b.wait()


def finish(c, r):
    c = pltpu.with_memory_space_constraint(c, pltpu.VMEM)
    r = pltpu.with_memory_space_constraint(r, pltpu.VMEM)
    return pl.pallas_call(
        write_out,
        out_shape=(jax.ShapeDtypeStruct(c.shape, c.dtype),) * 2,
        in_specs=[pl.BlockSpec(memory_space=pltpu.VMEM)] * 2,
        out_specs=(pl.BlockSpec(memory_space=pl.ANY),) * 2,
        scratch_shapes=[pltpu.SemaphoreType.DMA((2,))],
        name="finish",
    )(c, r)


def per_device(h_blocks, p_blocks, p1_blocks, h_mask, p_mask, p1_mask):
    values = [v[:, 0] for v in (h_blocks, p1_blocks, p_blocks)]
    masks = [v[:, 0].T for v in (h_mask, p1_mask, p_mask)]
    return tuple(v[:, None] for v in finish(*exchange(values, masks)))


def solution(mesh):
    blocks = P(None, "row", "col", None, None)
    masks = P(None, "row", "col")
    return jax.shard_map(
        per_device, mesh=mesh, in_specs=(blocks,) * 3 + (masks,) * 3,
        out_specs=(blocks, blocks), check_vma=False,
    )
```

```python
import functools

import jax
import jax.numpy as jnp
from jax import lax
from jax.experimental import pallas as pl
from jax.experimental.pallas import tpu as pltpu
from jax.sharding import PartitionSpec as P

MESH = pl.DeviceIdType.MESH
NX, NY, NZ, NC = 4, 4, 8, 2
NM = 4
M, O = 0, 1
UP_HOPS = (4, 3)
DOWN_HOPS = (3, 4)


FINE = ((False, 3, O), (True, 4, M), (False, 4, O))
LAST = FINE[1:]
WHOLE = tuple((up, hop, kind) for up in (True, False) for kind in (M, O)
              for hop in range(1, (UP_HOPS if up else DOWN_HOPS)[kind] + 1) if (up, hop, kind) not in FINE)


def kernel(h_ref, p1_ref, p_ref, h_hbm, p1_hbm, p_hbm, out_c, out_r,
           masks, raw, strip, left, far, out_f, back, acc,
           whole_recv, fine_recv, last_recv, f_recv, l_recv, c_recv, p_recv, r_recv,
           z_send, y_send, c_send, f_send, p_send, q_send, fy_send, r_send, local_sem):
    row, col = lax.axis_index("row"), lax.axis_index("col")
    x, z = row // NZ, row % NZ
    y, k = col // NC, col % NC
    u = col
    low = z <= u
    x_up, x_dn = (x + 1) % NX, (x + NX - 1) % NX
    z_up, z_dn = (z + 1) % NZ, (z + NZ - 1) % NZ
    y_up, y_dn = (y + 1) % NY, (y + NY - 1) % NY

    def dev(x_=x, y_=y, z_=z, k_=k):
        return (x_ * NZ + z_, y_ * NC + k_)

    dev_zu, dev_zd = dev(z_=z_up), dev(z_=z_dn)
    dev_yu, dev_yd = dev(y_=y_up), dev(y_=y_dn)
    dev_xu, dev_xd = dev(x_=x_up), dev(x_=x_dn)
    dev_c = dev(k_=1 - k)

    def remote(src, dst, send, recv, device):
        return pltpu.make_async_remote_copy(
            src_ref=src, dst_ref=dst, send_sem=send, recv_sem=recv,
            device_id=device, device_id_type=MESH)

    for i, ref in enumerate((h_ref, p1_ref, p_ref)):
        pltpu.make_async_copy(ref, raw.at[i], local_sem.at[0]).start()
    for i, ref in enumerate((h_hbm, p1_hbm, p_hbm)):
        pltpu.make_async_copy(ref, masks.at[i], local_sem.at[1]).start()
    barrier = pltpu.get_barrier_semaphore()
    for peer in (dev_zu, dev_zd, dev_yu, dev_yd, dev_xu, dev_xd, dev_c):
        pl.semaphore_signal(barrier, inc=1, device_id=peer, device_id_type=MESH)

    slot_m = jnp.where(low, 1, 0)
    slots = (slot_m, 1 - slot_m)
    own = left.at[u]

    def keep_own(kind):
        for i in range(3):
            for m in range(NM):
                keep = jnp.full((128, 128), masks[i, slots[kind], m].astype(jnp.float32)).astype(jnp.bfloat16)
                block = raw[i, m, slots[kind]] * keep
                left[u, kind, m, i] = block
                if kind == M:
                    strip[z, M, m, i] = block

    pltpu.make_async_copy(masks, masks, local_sem.at[1]).wait()
    pltpu.make_async_copy(raw, raw, local_sem.at[0]).wait()
    keep_own(M)
    pl.semaphore_wait(barrier, 7)

    def z_from(up, hop):
        return (z - hop + NZ) % NZ if up else (z + hop) % NZ

    def z_sem(up, hop, kind, m):
        key = (up, hop, kind)
        return fine_recv.at[FINE.index(key), m] if key in FINE else whole_recv.at[WHOLE.index(key)]

    def z_copy(up, hop, kind, m):
        spot = strip.at[z_from(up, hop), kind, m]
        return remote(spot, spot, z_send, z_sem(up, hop + 1, kind, m), dev_zu if up else dev_zd)

    def z_wait(up, hop, kind, m=None):
        spot = strip.at[z_from(up, hop), kind] if m is None else strip.at[z_from(up, hop), kind, m]
        remote(spot, spot, z_send, z_sem(up, hop, kind, m), dev_c).wait_recv()

    def z_part(up, part, hop=3):
        kind = M if up else O
        spot = strip.at[z_from(up, hop), kind, NM - 1, pl.ds(2 * part, 2 - part)]
        sem = fine_recv.at[1 if up else 2, NM - 1] if part == 0 else last_recv.at[0 if up else 1]
        return remote(spot, spot, z_send, sem, dev_zu if up else dev_zd)

    def z_round(hop, kind, planes=range(NM)):
        for up in (True, False):
            limit = (UP_HOPS if up else DOWN_HOPS)[kind]
            if hop > limit:
                continue
            onward = hop < limit
            if (up, hop, kind) not in FINE and (0 if onward else NM - 1) in planes:
                z_wait(up, hop, kind)
            for m in planes:
                if (up, hop, kind) in FINE:
                    z_wait(up, hop, kind, m)
                if onward and m == NM - 1 and (up, hop + 1, kind) in LAST:
                    z_part(up, 0).start()
                    z_part(up, 1).start()
                elif onward:
                    z_copy(up, hop, kind, m).start()

    for m in range(NM):
        z_copy(True, 0, M, m).start()
        z_copy(False, 0, M, m).start()
    keep_own(O)

    dev_f = (jnp.where(low, x_dn, x_up) * NZ + z, col)
    shift_up = jnp.where(x == NX - 1, 1, 0)
    shift_dn = jnp.where(x == 0, NM - 1, 0)
    f_shift = jnp.where(low, shift_dn, shift_up)

    def f_copy(there):
        m = (there + NM - f_shift) % NM
        return remote(own.at[O, m], strip.at[z, O, there], f_send, f_recv.at[there], dev_f)

    for m in range(NM):
        f_copy(m).start()

    def l_wait(d, kind):
        spot = left.at[((y + d) % NY) * NC + k, kind]
        remote(spot, spot, y_send, l_recv.at[d - 1, kind], dev_c).wait_recv()

    def y_copy(up, kind, relay):
        if relay:
            who = (y_dn if up else y_up) * NC + k
            d = 2
        else:
            who = u
            d = 3 if up else 1
        spot = left.at[who, kind]
        return remote(spot, spot, y_send, l_recv.at[d - 1, kind], dev_yu if up else dev_yd)

    y_relays = [y_copy(True, M, True), y_copy(False, O, True)]
    for up, kind in ((True, M), (False, O), (True, O), (False, M)):
        y_copy(up, kind, False).start()

    def c_copy(d, kind):
        spot = left.at[((y + d) % NY) * NC + k, kind]
        return remote(spot, spot, c_send, c_recv, dev_c)

    c_copy(0, M).start()
    c_copy(0, O).start()

    def far_wanted(side, who, kind, at):
        if side == 0:
            inside = who >= z if kind == O else who <= 2 * at + 1
            return jnp.logical_and(2 * at + 1 >= z, inside)
        inside = who < z if kind == O else who > 2 * at
        return jnp.logical_and(2 * at < z, inside)

    def twin(side, who, kind):
        return jnp.logical_and(who == 2 * y + 1, side == 1 and kind == M)

    def far_recv(side, who, kind):
        return p_recv.at[jnp.where(twin(side, who, kind), 16, kind * 8 + who)]

    def wait_count(conditions, sem):
        count = sum(jnp.where(c, 1, 0) for c in conditions)
        for n in range(1, 9):
            @pl.when(count == n)
            def _():
                some = far.at[0, pl.ds(0, n), M]
                remote(some, some, sem, f_recv.at[0], dev_c).wait_send()

    def far_by_x(side, d, kind):
        home = (y + d) % NY
        who = home * NC + k
        wanted = far_wanted(side, who, kind, y)
        if d in (1, 3):
            wanted = jnp.logical_and(wanted, jnp.logical_not(far_wanted(side, who, kind, home)))
        return wanted

    def far_sends(d, kind):
        who = ((y + d) % NY) * NC + k
        src = left.at[who, kind]
        for side in (0, 1):
            @pl.when(far_by_x(side, d, kind))
            def _():
                shift = shift_dn if side == 0 else shift_up
                for m in range(NM):
                    remote(src.at[m], far.at[side, who, kind, (m + shift) % NM], p_send, far_recv(side, who, kind),
                           dev_xd if side == 0 else dev_xu).start()

    def far_by_y(side, kind, there):
        return jnp.logical_and(far_wanted(side, u, kind, y), far_wanted(side, u, kind, there))

    def far_y(kind):
        for side in (0, 1):
            for there, device in ((y_up, dev_yu), (y_dn, dev_yd)):
                @pl.when(far_by_y(side, kind, there))
                def _():
                    src = strip.at[z, O] if kind == O else far.at[side, u, M]
                    remote(src, far.at[side, u, kind], fy_send, p_recv.at[kind * 8 + u], device).start()

    def far_pass(d, kind):
        who = ((y + d) % NY) * NC + k
        for side in (0, 1):
            @pl.when(far_wanted(side, who, kind, y))
            def _():
                spot = far.at[side, who, kind]
                copy = remote(spot, spot, q_send, far_recv(side, who, kind), dev_c)
                copy.wait_recv()
                copy.start()

    side_f = jnp.where(low, 0, 1)
    far_sends(0, M)

    for m in range(NM):
        acc[m] = jnp.zeros((2, 2, 128, 128), jnp.float32)

    for m in range(NM):
        remote(strip.at[z, O, m], strip.at[z, O, m], f_send, f_recv.at[m], dev_c).wait_recv()
        z_copy(True, 0, O, m).start()
        z_copy(False, 0, O, m).start()
    f_keep = pltpu.make_async_copy(strip.at[z, O], far.at[side_f, u, O], local_sem.at[2])
    f_keep.start()
    f_pass = remote(strip.at[z, O], far.at[side_f, u, O], local_sem.at[3], p_recv.at[8 + u], dev_c)
    f_pass.start()

    l_wait(3, M)
    y_relays[0].start()
    far_sends(3, M)
    c_copy(3, M).start()
    l_wait(1, O)
    y_relays[1].start()
    far_sends(1, O)
    c_copy(1, O).start()
    far_y(O)

    z_round(1, M)

    l_wait(3, O)
    far_sends(3, O)
    c_copy(3, O).start()
    l_wait(1, M)
    far_sends(1, M)
    c_copy(1, M).start()

    far_pass(0, M)
    far_y(M)
    z_round(1, O)
    z_round(2, M)

    l_wait(2, M)
    far_sends(2, M)
    c_copy(2, M).start()
    l_wait(2, O)
    far_sends(2, O)
    c_copy(2, O).start()

    z_round(2, O)
    far_pass(3, O)
    far_pass(1, O)

    zero = jnp.zeros((128, 128), jnp.bfloat16)

    def sides(r, m, zp, which):
        if r == 0:
            ok = jnp.where(zp > u, zp >= z, zp < z)
            first = {i: left[zp, M, m, i] for i in which}
            second = {i: jnp.where(ok, left[zp, O, m, i], zero) for i in which}
        else:
            ok_m = jnp.where(low, zp >= z, zp < z)
            ok_f = (zp <= u) == low
            first = {i: jnp.where(ok_m, far[side_f, zp, O, m, i], zero) for i in which}
            second = {i: jnp.where(ok_f, far[side_f, zp, M, m, i], zero) for i in which}
        return {i: jnp.concatenate([first[i], second[i]], axis=1) for i in which}

    def products(r, m, zp):
        hm, am, pm = (strip[zp, M, m, i] for i in range(3))
        hf, af, pf = (strip[zp, O, m, i] for i in range(3))
        lhs = sides(r, m, zp, (0, 1, 2))
        one = jnp.dot(jnp.concatenate([lhs[0], lhs[2]], axis=0), jnp.concatenate([am, af], axis=0),
                      preferred_element_type=jnp.float32)
        rhs = jnp.concatenate([jnp.concatenate([-hm, pm], axis=1), jnp.concatenate([-hf, pf], axis=1)], axis=0)
        two = jnp.dot(lhs[1], rhs, preferred_element_type=jnp.float32)
        return one[:128] + two[:, :128], one[128:] + two[:, 128:]

    def one_product(r, m, zp, i):
        lhs = sides(r, m, zp, (i, 1))
        bm, am, bf, af = strip[zp, M, m, i], strip[zp, M, m, 1], strip[zp, O, m, i], strip[zp, O, m, 1]
        if i == 0:
            bm, bf = -bm, -bf
        return jnp.dot(jnp.concatenate([lhs[i], lhs[1]], axis=1), jnp.concatenate([am, af, bm, bf], axis=0),
                       preferred_element_type=jnp.float32)

    def add(r, m, zp):
        c, s = products(r, m, zp)
        acc[m, r, 0] += c
        acc[m, r, 1] += s

    halves = left.at[pl.ds(0, NY)]
    remote(halves, halves, c_send, c_recv, dev_c).wait_recv()

    def near(i, _):
        add(0, i // 5, (z + i % 5 + 6) % NZ)
        return 0

    lax.fori_loop(0, NM * 5, near, 0)

    z_round(3, M)
    far_pass(3, M)
    far_pass(1, M)
    far_pass(2, M)
    z_round(3, O, (0, 1))
    far_pass(2, O)
    f_keep.wait()
    for d in range(NY):
        who = ((y + d) % NY) * NC + 1 - k
        for kind in (M, O):
            for side in (0, 1):
                @pl.when(far_wanted(side, who, kind, y))
                def _():
                    spot = far.at[side, who, kind]
                    remote(spot, spot, q_send, far_recv(side, who, kind), dev_c).wait_recv()

    def far_near(i, _):
        add(1, i // 5, (z + i % 5 + 6) % NZ)
        return 0

    lax.fori_loop(0, 10, far_near, 0)
    z_round(3, O, (2,))
    lax.fori_loop(10, 15, far_near, 0)
    z_round(3, O, (3,))
    lax.fori_loop(15, 20, far_near, 0)

    r_shift = jnp.where(low, shift_up, shift_dn)
    b_shift = jnp.where(low, jnp.where(x == 0, 1, 0), jnp.where(x == NX - 1, NM - 1, 0))
    dev_r = (jnp.where(low, x_up, x_dn) * NZ + z, col)

    def r_copy(m):
        there = (m + r_shift) % NM
        return remote(out_f.at[m], back.at[there], r_send, r_recv.at[m], dev_r)

    def r_part(i):
        there = (NM - 1 + r_shift) % NM
        return remote(out_f.at[NM - 1, i], back.at[there, i], r_send, r_recv.at[NM - 1 + i], dev_r)

    def put(m, kind, c, s):
        keep = masks[1, slots[kind], m].astype(jnp.float32)
        out_c[m, slots[kind]] = (c * keep).astype(jnp.bfloat16)
        out_r[m, slots[kind]] = (s * keep).astype(jnp.bfloat16)

    for m in range(NM):
        def third(i, _):
            add(0, m, (z + 3 + 2 * i) % NZ)
            add(1, m, (z + 3 + 2 * i) % NZ)
            return 0

        lax.fori_loop(0, 2, third, 0)
        opposite = (z + 4) % NZ
        if m < NM - 1:
            z_wait(True, 4, M, m)
            z_wait(False, 4, O, m)
            c, s = products(1, m, opposite)
            out_f[m, 0] = (c + acc[m, 1, 0]).astype(jnp.bfloat16)
            out_f[m, 1] = (s + acc[m, 1, 1]).astype(jnp.bfloat16)
            c, s = products(0, m, opposite)
            put(m, M, c + acc[m, 0, 0], s + acc[m, 0, 1])
            r_copy(m).start()
        else:
            total = []
            for i in range(2):
                for up in (True, False):
                    z_part(up, i, 4).wait_recv()
                out_f[m, i] = (one_product(1, m, opposite, 2 * i) + acc[m, 1, i]).astype(jnp.bfloat16)
                total.append(one_product(0, m, opposite, 2 * i) + acc[m, 0, i])
                r_part(i).start()
            put(m, M, *total)

    def sent_all(ref, sem):
        remote(ref, ref, sem, r_recv.at[0], dev_c).wait_send()

    sent_all(strip.at[pl.ds(0, NZ - 1)], z_send)
    sent_all(left.at[pl.ds(0, 3)], y_send)
    sent_all(left.at[pl.ds(0, NY)], c_send)
    sent_all(strip.at[0, O], f_send)
    sent_all(strip.at[0, O], local_sem.at[3])
    own_chunks = [(d, kind) for d in range(NY) for kind in (M, O) if (d, kind) != (0, O)]
    wait_count([far_by_y(side, kind, there) for side in (0, 1) for kind in (M, O) for there in (y_up, y_dn)], fy_send)
    wait_count([far_by_x(side, d, kind) for side in (0, 1) for d, kind in own_chunks], p_send)
    wait_count([far_wanted(side, ((y + d) % NY) * NC + k, kind, y) for side in (0, 1) for d, kind in own_chunks],
               q_send)

    for sent in range(NM):
        m = (sent + b_shift) % NM
        if sent < NM - 1:
            remote(back.at[m], back.at[m], r_send, r_recv.at[sent], dev_c).wait_recv()
        else:
            for i in range(2):
                remote(back.at[m, i], back.at[m, i], r_send, r_recv.at[sent + i], dev_c).wait_recv()
        put(m, O, back[m, 0].astype(jnp.float32), back[m, 1].astype(jnp.float32))
    sent_all(out_f, r_send)


def exchange(values, masks):
    dma = pltpu.SemaphoreType.DMA
    block = (128, 128)
    return pl.pallas_call(
        kernel,
        out_shape=(pltpu.VMEM((NM, 2) + block, jnp.bfloat16),) * 2,
        in_specs=[pl.BlockSpec(memory_space=pl.ANY)] * 6,
        out_specs=(pl.BlockSpec(memory_space=pltpu.VMEM),) * 2,
        scratch_shapes=[
            pltpu.SMEM((3, 2, NM), jnp.int32),
            pltpu.VMEM((3, NM, 2) + block, jnp.bfloat16),
            pltpu.VMEM((NZ, 2, NM, 3) + block, jnp.bfloat16),
            pltpu.VMEM((8, 2, NM, 3) + block, jnp.bfloat16),
            pltpu.VMEM((2, 8, 2, NM, 3) + block, jnp.bfloat16),
            pltpu.VMEM((NM, 2) + block, jnp.bfloat16),
            pltpu.VMEM((NM, 2) + block, jnp.bfloat16),
            pltpu.VMEM((NM, 2, 2) + block, jnp.float32),
            dma((len(WHOLE),)),
            dma((len(FINE), NM)),
            dma((2,)),
            dma((NM,)),
            dma((NY - 1, 2)),
            dma(()),
            dma((17,)),
            dma((NM + 1,)),
            dma(()),
            dma(()),
            dma(()),
            dma(()),
            dma(()),
            dma(()),
            dma(()),
            dma(()),
            dma((4,)),
        ],
        compiler_params=pltpu.CompilerParams(collective_id=0, has_side_effects=True),
        name="exchange",
    )(*values, *masks)


def write_out(c_ref, r_ref, oc, orr, sem):
    a = pltpu.make_async_copy(c_ref, oc, sem.at[0])
    b = pltpu.make_async_copy(r_ref, orr, sem.at[1])
    a.start()
    b.start()
    a.wait()
    b.wait()


def finish(c, r):
    c = pltpu.with_memory_space_constraint(c, pltpu.VMEM)
    r = pltpu.with_memory_space_constraint(r, pltpu.VMEM)
    return pl.pallas_call(
        write_out,
        out_shape=(jax.ShapeDtypeStruct(c.shape, c.dtype),) * 2,
        in_specs=[pl.BlockSpec(memory_space=pltpu.VMEM)] * 2,
        out_specs=(pl.BlockSpec(memory_space=pl.ANY),) * 2,
        scratch_shapes=[pltpu.SemaphoreType.DMA((2,))],
        name="finish",
    )(c, r)


def per_device(h_blocks, p_blocks, p1_blocks, h_mask, p_mask, p1_mask):
    values = [v[:, 0] for v in (h_blocks, p1_blocks, p_blocks)]
    masks = [v[:, 0].T for v in (h_mask, p1_mask, p_mask)]
    return tuple(v[:, None] for v in finish(*exchange(values, masks)))


def solution(mesh):
    blocks = P(None, "row", "col", None, None)
    masks = P(None, "row", "col")
    return jax.shard_map(
        per_device, mesh=mesh, in_specs=(blocks,) * 3 + (masks,) * 3,
        out_specs=(blocks, blocks), check_vma=False,
    )
```

```python
import functools

import jax
import jax.numpy as jnp
from jax import lax
from jax.experimental import pallas as pl
from jax.experimental.pallas import tpu as pltpu
from jax.sharding import PartitionSpec as P

MESH = pl.DeviceIdType.MESH
NX, NY, NZ, NC = 4, 4, 8, 2
NM = 4
M, O = 0, 1
UP_HOPS = (4, 3)
DOWN_HOPS = (3, 4)


FINE = ((False, 3, O), (True, 4, M), (False, 4, O))
LAST = FINE[1:]
WHOLE = tuple((up, hop, kind) for up in (True, False) for kind in (M, O)
              for hop in range(1, (UP_HOPS if up else DOWN_HOPS)[kind] + 1) if (up, hop, kind) not in FINE)


def kernel(h_ref, p1_ref, p_ref, h_hbm, p1_hbm, p_hbm, out_c, out_r,
           masks, raw, strip, left, far, out_f, back, acc,
           whole_recv, fine_recv, last_recv, f_recv, l_recv, c_recv, p_recv, r_recv,
           z_send, y_send, c_send, f_send, p_send, q_send, fy_send, r_send, local_sem):
    row, col = lax.axis_index("row"), lax.axis_index("col")
    x, z = row // NZ, row % NZ
    y, k = col // NC, col % NC
    u = col
    low = z <= u
    x_up, x_dn = (x + 1) % NX, (x + NX - 1) % NX
    z_up, z_dn = (z + 1) % NZ, (z + NZ - 1) % NZ
    y_up, y_dn = (y + 1) % NY, (y + NY - 1) % NY

    def dev(x_=x, y_=y, z_=z, k_=k):
        return (x_ * NZ + z_, y_ * NC + k_)

    dev_zu, dev_zd = dev(z_=z_up), dev(z_=z_dn)
    dev_yu, dev_yd = dev(y_=y_up), dev(y_=y_dn)
    dev_xu, dev_xd = dev(x_=x_up), dev(x_=x_dn)
    dev_c = dev(k_=1 - k)

    def remote(src, dst, send, recv, device):
        return pltpu.make_async_remote_copy(
            src_ref=src, dst_ref=dst, send_sem=send, recv_sem=recv,
            device_id=device, device_id_type=MESH)

    for i, ref in enumerate((h_ref, p1_ref, p_ref)):
        pltpu.make_async_copy(ref, raw.at[i], local_sem.at[0]).start()
    for i, ref in enumerate((h_hbm, p1_hbm, p_hbm)):
        pltpu.make_async_copy(ref, masks.at[i], local_sem.at[1]).start()
    barrier = pltpu.get_barrier_semaphore()
    for peer in (dev_zu, dev_zd, dev_yu, dev_yd, dev_xu, dev_xd, dev_c):
        pl.semaphore_signal(barrier, inc=1, device_id=peer, device_id_type=MESH)

    slot_m = jnp.where(low, 1, 0)
    slots = (slot_m, 1 - slot_m)
    own = left.at[u]

    def keep_own(kind):
        for i in range(3):
            for m in range(NM):
                keep = jnp.full((128, 128), masks[i, slots[kind], m].astype(jnp.float32)).astype(jnp.bfloat16)
                block = raw[i, m, slots[kind]] * keep
                left[u, kind, m, i] = block
                if kind == M:
                    strip[z, M, m, i] = block

    pltpu.make_async_copy(masks, masks, local_sem.at[1]).wait()
    pltpu.make_async_copy(raw, raw, local_sem.at[0]).wait()
    keep_own(M)
    pl.semaphore_wait(barrier, 7)

    def z_from(up, hop):
        return (z - hop + NZ) % NZ if up else (z + hop) % NZ

    def z_sem(up, hop, kind, m):
        key = (up, hop, kind)
        return fine_recv.at[FINE.index(key), m] if key in FINE else whole_recv.at[WHOLE.index(key)]

    def z_copy(up, hop, kind, m):
        spot = strip.at[z_from(up, hop), kind, m]
        return remote(spot, spot, z_send, z_sem(up, hop + 1, kind, m), dev_zu if up else dev_zd)

    def z_wait(up, hop, kind, m=None):
        spot = strip.at[z_from(up, hop), kind] if m is None else strip.at[z_from(up, hop), kind, m]
        remote(spot, spot, z_send, z_sem(up, hop, kind, m), dev_c).wait_recv()

    def z_part(up, part, hop=3):
        kind = M if up else O
        spot = strip.at[z_from(up, hop), kind, NM - 1, pl.ds(2 * part, 2 - part)]
        sem = fine_recv.at[1 if up else 2, NM - 1] if part == 0 else last_recv.at[0 if up else 1]
        return remote(spot, spot, z_send, sem, dev_zu if up else dev_zd)

    def z_round(hop, kind, planes=range(NM)):
        for up in (True, False):
            limit = (UP_HOPS if up else DOWN_HOPS)[kind]
            if hop > limit:
                continue
            onward = hop < limit
            if (up, hop, kind) not in FINE and (0 if onward else NM - 1) in planes:
                z_wait(up, hop, kind)
            for m in planes:
                if (up, hop, kind) in FINE:
                    z_wait(up, hop, kind, m)
                if onward and m == NM - 1 and (up, hop + 1, kind) in LAST:
                    z_part(up, 0).start()
                    z_part(up, 1).start()
                elif onward:
                    z_copy(up, hop, kind, m).start()

    for m in range(NM):
        z_copy(True, 0, M, m).start()
        z_copy(False, 0, M, m).start()
    keep_own(O)

    dev_f = (jnp.where(low, x_dn, x_up) * NZ + z, col)
    shift_up = jnp.where(x == NX - 1, 1, 0)
    shift_dn = jnp.where(x == 0, NM - 1, 0)
    f_shift = jnp.where(low, shift_dn, shift_up)

    def f_copy(there):
        m = (there + NM - f_shift) % NM
        return remote(own.at[O, m], strip.at[z, O, there], f_send, f_recv.at[there], dev_f)

    for m in range(NM):
        f_copy(m).start()

    def l_wait(d, kind):
        spot = left.at[((y + d) % NY) * NC + k, kind]
        remote(spot, spot, y_send, l_recv.at[d - 1, kind], dev_c).wait_recv()

    def y_copy(up, kind, relay):
        if relay:
            who = (y_dn if up else y_up) * NC + k
            d = 2
        else:
            who = u
            d = 3 if up else 1
        spot = left.at[who, kind]
        return remote(spot, spot, y_send, l_recv.at[d - 1, kind], dev_yu if up else dev_yd)

    y_relays = [y_copy(True, M, True), y_copy(False, O, True)]
    for up, kind in ((True, M), (False, O), (True, O), (False, M)):
        y_copy(up, kind, False).start()

    def c_copy(d, kind):
        spot = left.at[((y + d) % NY) * NC + k, kind]
        return remote(spot, spot, c_send, c_recv, dev_c)

    c_copy(0, M).start()
    c_copy(0, O).start()

    def far_wanted(side, who, kind, at):
        if side == 0:
            inside = who >= z if kind == O else who <= 2 * at + 1
            return jnp.logical_and(2 * at + 1 >= z, inside)
        inside = who < z if kind == O else who > 2 * at
        return jnp.logical_and(2 * at < z, inside)

    def twin(side, who, kind):
        return jnp.logical_and(who == 2 * y + 1, side == 1 and kind == M)

    def far_recv(side, who, kind):
        return p_recv.at[jnp.where(twin(side, who, kind), 16, kind * 8 + who)]

    def wait_count(conditions, sem):
        count = sum(jnp.where(c, 1, 0) for c in conditions)
        for n in range(1, 9):
            @pl.when(count == n)
            def _():
                some = far.at[0, pl.ds(0, n), M]
                remote(some, some, sem, f_recv.at[0], dev_c).wait_send()

    def far_by_x(side, d, kind):
        home = (y + d) % NY
        who = home * NC + k
        wanted = far_wanted(side, who, kind, y)
        if d in (1, 3):
            wanted = jnp.logical_and(wanted, jnp.logical_not(far_wanted(side, who, kind, home)))
        return wanted

    def far_sends(d, kind):
        who = ((y + d) % NY) * NC + k
        src = left.at[who, kind]
        for side in (0, 1):
            @pl.when(far_by_x(side, d, kind))
            def _():
                shift = shift_dn if side == 0 else shift_up
                for m in range(NM):
                    remote(src.at[m], far.at[side, who, kind, (m + shift) % NM], p_send, far_recv(side, who, kind),
                           dev_xd if side == 0 else dev_xu).start()

    def far_by_y(side, kind, there):
        return jnp.logical_and(far_wanted(side, u, kind, y), far_wanted(side, u, kind, there))

    def far_y(kind):
        for side in (0, 1):
            for there, device in ((y_up, dev_yu), (y_dn, dev_yd)):
                @pl.when(far_by_y(side, kind, there))
                def _():
                    src = strip.at[z, O] if kind == O else far.at[side, u, M]
                    remote(src, far.at[side, u, kind], fy_send, p_recv.at[kind * 8 + u], device).start()

    def far_pass(d, kind):
        who = ((y + d) % NY) * NC + k
        for side in (0, 1):
            @pl.when(far_wanted(side, who, kind, y))
            def _():
                spot = far.at[side, who, kind]
                copy = remote(spot, spot, q_send, far_recv(side, who, kind), dev_c)
                copy.wait_recv()
                copy.start()

    side_f = jnp.where(low, 0, 1)
    far_sends(0, M)

    for m in range(NM):
        acc[m] = jnp.zeros((2, 2, 128, 128), jnp.float32)

    for m in range(NM):
        remote(strip.at[z, O, m], strip.at[z, O, m], f_send, f_recv.at[m], dev_c).wait_recv()
        z_copy(True, 0, O, m).start()
        z_copy(False, 0, O, m).start()
    f_keep = pltpu.make_async_copy(strip.at[z, O], far.at[side_f, u, O], local_sem.at[2])
    f_keep.start()
    f_pass = remote(strip.at[z, O], far.at[side_f, u, O], local_sem.at[3], p_recv.at[8 + u], dev_c)
    f_pass.start()

    l_wait(3, M)
    y_relays[0].start()
    far_sends(3, M)
    c_copy(3, M).start()
    l_wait(1, O)
    y_relays[1].start()
    far_sends(1, O)
    c_copy(1, O).start()
    far_y(O)

    z_round(1, M)

    l_wait(3, O)
    far_sends(3, O)
    c_copy(3, O).start()
    l_wait(1, M)
    far_sends(1, M)
    c_copy(1, M).start()

    far_pass(0, M)
    far_y(M)
    z_round(1, O)
    z_round(2, M)

    l_wait(2, M)
    far_sends(2, M)
    c_copy(2, M).start()
    l_wait(2, O)
    far_sends(2, O)
    c_copy(2, O).start()

    z_round(2, O)
    far_pass(3, O)
    far_pass(1, O)

    zero = jnp.zeros((128, 128), jnp.bfloat16)

    def sides(r, m, zp, which):
        if r == 0:
            ok = jnp.where(zp > u, zp >= z, zp < z)
            first = {i: left[zp, M, m, i] for i in which}
            second = {i: jnp.where(ok, left[zp, O, m, i], zero) for i in which}
        else:
            ok_m = jnp.where(low, zp >= z, zp < z)
            ok_f = (zp <= u) == low
            first = {i: jnp.where(ok_m, far[side_f, zp, O, m, i], zero) for i in which}
            second = {i: jnp.where(ok_f, far[side_f, zp, M, m, i], zero) for i in which}
        return {i: jnp.concatenate([first[i], second[i]], axis=1) for i in which}

    def products(r, m, zp):
        hm, am, pm = (strip[zp, M, m, i] for i in range(3))
        hf, af, pf = (strip[zp, O, m, i] for i in range(3))
        lhs = sides(r, m, zp, (0, 1, 2))
        one = jnp.dot(jnp.concatenate([lhs[0], lhs[2]], axis=0), jnp.concatenate([am, af], axis=0),
                      preferred_element_type=jnp.float32)
        rhs = jnp.concatenate([jnp.concatenate([-hm, pm], axis=1), jnp.concatenate([-hf, pf], axis=1)], axis=0)
        two = jnp.dot(lhs[1], rhs, preferred_element_type=jnp.float32)
        return one[:128] + two[:, :128], one[128:] + two[:, 128:]

    def one_product(r, m, zp, i):
        lhs = sides(r, m, zp, (i, 1))
        bm, am, bf, af = strip[zp, M, m, i], strip[zp, M, m, 1], strip[zp, O, m, i], strip[zp, O, m, 1]
        if i == 0:
            bm, bf = -bm, -bf
        return jnp.dot(jnp.concatenate([lhs[i], lhs[1]], axis=1), jnp.concatenate([am, af, bm, bf], axis=0),
                       preferred_element_type=jnp.float32)

    def add(r, m, zp):
        c, s = products(r, m, zp)
        acc[m, r, 0] += c
        acc[m, r, 1] += s

    halves = left.at[pl.ds(0, NY)]
    remote(halves, halves, c_send, c_recv, dev_c).wait_recv()

    def near(i, _):
        add(0, i // 5, (z + i % 5 + 6) % NZ)
        return 0

    lax.fori_loop(0, NM * 5, near, 0)

    z_round(3, M)
    far_pass(3, M)
    far_pass(1, M)
    far_pass(2, M)
    z_round(3, O, (0, 1))
    far_pass(2, O)
    f_keep.wait()
    for d in range(NY):
        who = ((y + d) % NY) * NC + 1 - k
        for kind in (M, O):
            for side in (0, 1):
                @pl.when(far_wanted(side, who, kind, y))
                def _():
                    spot = far.at[side, who, kind]
                    remote(spot, spot, q_send, far_recv(side, who, kind), dev_c).wait_recv()

    def far_near(i, _):
        add(1, i // 5, (z + i % 5 + 6) % NZ)
        return 0

    lax.fori_loop(0, 10, far_near, 0)
    z_round(3, O, (2,))
    lax.fori_loop(10, 15, far_near, 0)
    z_round(3, O, (3,))
    lax.fori_loop(15, 20, far_near, 0)

    r_shift = jnp.where(low, shift_up, shift_dn)
    b_shift = jnp.where(low, jnp.where(x == 0, 1, 0), jnp.where(x == NX - 1, NM - 1, 0))
    dev_r = (jnp.where(low, x_up, x_dn) * NZ + z, col)

    def r_copy(m):
        there = (m + r_shift) % NM
        return remote(out_f.at[m], back.at[there], r_send, r_recv.at[m], dev_r)

    def r_part(i):
        there = (NM - 1 + r_shift) % NM
        return remote(out_f.at[NM - 1, i], back.at[there, i], r_send, r_recv.at[NM - 1 + i], dev_r)

    def put(m, kind, c, s):
        keep = masks[1, slots[kind], m].astype(jnp.float32)
        out_c[m, slots[kind]] = (c * keep).astype(jnp.bfloat16)
        out_r[m, slots[kind]] = (s * keep).astype(jnp.bfloat16)

    for m in range(NM):
        def third(i, _):
            add(0, m, (z + 3 + 2 * i) % NZ)
            add(1, m, (z + 3 + 2 * i) % NZ)
            return 0

        lax.fori_loop(0, 2, third, 0)
        opposite = (z + 4) % NZ
        if m < NM - 1:
            z_wait(True, 4, M, m)
            z_wait(False, 4, O, m)
            c, s = products(1, m, opposite)
            out_f[m, 0] = (c + acc[m, 1, 0]).astype(jnp.bfloat16)
            out_f[m, 1] = (s + acc[m, 1, 1]).astype(jnp.bfloat16)
            c, s = products(0, m, opposite)
            put(m, M, c + acc[m, 0, 0], s + acc[m, 0, 1])
            r_copy(m).start()
        else:
            def half(r, i, j):
                return jnp.dot(sides(r, m, opposite, (i,))[i],
                               jnp.concatenate([strip[opposite, M, m, j], strip[opposite, O, m, j]], axis=0),
                               preferred_element_type=jnp.float32)

            for up in (True, False):
                z_part(up, 0, 4).wait_recv()
            out_f[m, 0] = (one_product(1, m, opposite, 0) + acc[m, 1, 0]).astype(jnp.bfloat16)
            total = [one_product(0, m, opposite, 0) + acc[m, 0, 0]]
            r_part(0).start()
            for r in range(2):
                acc[m, r, 1] += half(r, 2, 1)
            for up in (True, False):
                z_part(up, 1, 4).wait_recv()
            out_f[m, 1] = (half(1, 1, 2) + acc[m, 1, 1]).astype(jnp.bfloat16)
            total.append(half(0, 1, 2) + acc[m, 0, 1])
            r_part(1).start()
            put(m, M, *total)

    def sent_all(ref, sem):
        remote(ref, ref, sem, r_recv.at[0], dev_c).wait_send()

    sent_all(strip.at[pl.ds(0, NZ - 1)], z_send)
    sent_all(left.at[pl.ds(0, 3)], y_send)
    sent_all(left.at[pl.ds(0, NY)], c_send)
    sent_all(strip.at[0, O], f_send)
    sent_all(strip.at[0, O], local_sem.at[3])
    own_chunks = [(d, kind) for d in range(NY) for kind in (M, O) if (d, kind) != (0, O)]
    wait_count([far_by_y(side, kind, there) for side in (0, 1) for kind in (M, O) for there in (y_up, y_dn)], fy_send)
    wait_count([far_by_x(side, d, kind) for side in (0, 1) for d, kind in own_chunks], p_send)
    wait_count([far_wanted(side, ((y + d) % NY) * NC + k, kind, y) for side in (0, 1) for d, kind in own_chunks],
               q_send)

    for sent in range(NM):
        m = (sent + b_shift) % NM
        if sent < NM - 1:
            remote(back.at[m], back.at[m], r_send, r_recv.at[sent], dev_c).wait_recv()
        else:
            for i in range(2):
                remote(back.at[m, i], back.at[m, i], r_send, r_recv.at[sent + i], dev_c).wait_recv()
        put(m, O, back[m, 0].astype(jnp.float32), back[m, 1].astype(jnp.float32))
    sent_all(out_f, r_send)


def exchange(values, masks):
    dma = pltpu.SemaphoreType.DMA
    block = (128, 128)
    return pl.pallas_call(
        kernel,
        out_shape=(pltpu.VMEM((NM, 2) + block, jnp.bfloat16),) * 2,
        in_specs=[pl.BlockSpec(memory_space=pl.ANY)] * 6,
        out_specs=(pl.BlockSpec(memory_space=pltpu.VMEM),) * 2,
        scratch_shapes=[
            pltpu.SMEM((3, 2, NM), jnp.int32),
            pltpu.VMEM((3, NM, 2) + block, jnp.bfloat16),
            pltpu.VMEM((NZ, 2, NM, 3) + block, jnp.bfloat16),
            pltpu.VMEM((8, 2, NM, 3) + block, jnp.bfloat16),
            pltpu.VMEM((2, 8, 2, NM, 3) + block, jnp.bfloat16),
            pltpu.VMEM((NM, 2) + block, jnp.bfloat16),
            pltpu.VMEM((NM, 2) + block, jnp.bfloat16),
            pltpu.VMEM((NM, 2, 2) + block, jnp.float32),
            dma((len(WHOLE),)),
            dma((len(FINE), NM)),
            dma((2,)),
            dma((NM,)),
            dma((NY - 1, 2)),
            dma(()),
            dma((17,)),
            dma((NM + 1,)),
            dma(()),
            dma(()),
            dma(()),
            dma(()),
            dma(()),
            dma(()),
            dma(()),
            dma(()),
            dma((4,)),
        ],
        compiler_params=pltpu.CompilerParams(collective_id=0, has_side_effects=True),
        name="exchange",
    )(*values, *masks)


def write_out(c_ref, r_ref, oc, orr, sem):
    a = pltpu.make_async_copy(c_ref, oc, sem.at[0])
    b = pltpu.make_async_copy(r_ref, orr, sem.at[1])
    a.start()
    b.start()
    a.wait()
    b.wait()


def finish(c, r):
    c = pltpu.with_memory_space_constraint(c, pltpu.VMEM)
    r = pltpu.with_memory_space_constraint(r, pltpu.VMEM)
    return pl.pallas_call(
        write_out,
        out_shape=(jax.ShapeDtypeStruct(c.shape, c.dtype),) * 2,
        in_specs=[pl.BlockSpec(memory_space=pltpu.VMEM)] * 2,
        out_specs=(pl.BlockSpec(memory_space=pl.ANY),) * 2,
        scratch_shapes=[pltpu.SemaphoreType.DMA((2,))],
        name="finish",
    )(c, r)


def per_device(h_blocks, p_blocks, p1_blocks, h_mask, p_mask, p1_mask):
    values = [v[:, 0] for v in (h_blocks, p1_blocks, p_blocks)]
    masks = [v[:, 0].T for v in (h_mask, p1_mask, p_mask)]
    return tuple(v[:, None] for v in finish(*exchange(values, masks)))


def solution(mesh):
    blocks = P(None, "row", "col", None, None)
    masks = P(None, "row", "col")
    return jax.shard_map(
        per_device, mesh=mesh, in_specs=(blocks,) * 3 + (masks,) * 3,
        out_specs=(blocks, blocks), check_vma=False,
    )
```
